32 devices in a mesh: groups: 2 (over x), gx: 16 (over z, y, core).
Axes of the slice: x: 2, y: 2, z: 4, core: 2. Of those that a mesh axis runs over, the one named last changes fastest.
Arguments:
- velocity: bfloat16 [3, 16, 128, 128], P(None, 'groups', 'gx'), parts along dimension 1, may hold values from -5 to 5
- offsets: int32 [6], P('groups'), parts along dimension 0, may hold values from 0 to 1023
- conv_in: bfloat16 [64, 9, 3, 3], replicated, may hold values from -0.625 to 0.625
- conv_mid: bfloat16 [64, 64, 3, 3], replicated, may hold values from -0.25 to 0.25
- conv_out: bfloat16 [36, 64, 3, 3], replicated, may hold values from -0.25 to 0.25
- cotangent: float32 [3, 8, 128, 128], P(None, 'groups', 'gx'), parts along dimension 1, may hold values from -6 to 6
Outputs:
- final_state: float32 [3, 8, 128, 128], P(None, 'groups', 'gx'), parts along dimension 1
- weight_grads: bfloat16 [36, 8, 128, 128], P(None, 'groups', 'gx'), parts along dimension 1
The draws below stay inside these ranges and needn't reach their ends.
There are 2 independent parts, one for each index of `groups`. The reference program is written for one: setup_inputs(seed, part) draws one part's arguments, and reference() takes and returns one part's arrays. A program takes and returns all parts, laid end to end along the dimension named above; an argument that names none is the same for every part. Nothing has to cross between parts.
All inputs are finite; a program needn't handle non-finite values.
Results may differ from the reference program's by a relative error of at most 0.0045.
Values may be sent and summed in bfloat16 or wider, within the bound.
No kernel may reach another device: no remote copies, remote signals or barrier semaphores. Data moves between devices by JAX's collectives and lax.ppermute only.
A program may use at most 128 MiB of HBM per device.

```python
import math
import jax
import jax.numpy as jnp
from jax import lax

NZ = 4
HIDDEN_SIZE = 64
STENCIL = 12
CHANNELS = 9
DOMAIN = 1024
NX = 128
NY = 128


def shard_levels(stream_key, dims, split, smallest, largest):
    def one(dim, blocks):
        heights = jax.random.uniform(jax.random.fold_in(jax.random.fold_in(stream_key, 6), dim), (blocks,), jnp.float32, smallest / len(split), largest / len(split))
        return jnp.repeat(jnp.exp(heights), dims[dim] // blocks).reshape((-1,) + (1,) * (len(dims) - dim - 1))

    factor_of = one(*split[0])
    for cut in split[1:]:
        factor_of = factor_of * one(*cut)
    return factor_of


def centred(own_key, shape, deviation, most, split=(), kind=jnp.bfloat16):
    gain = shard_levels(own_key, shape, split, -0.22, 0.18) if split else 1.0
    values = jax.random.normal(own_key, shape, jnp.float32) * deviation * gain
    return jnp.minimum(jnp.maximum(values, -most), most).astype(kind)


def setup_inputs(seed: int = 0, part: int = 0) -> dict:
    key_of = jax.random.split(jax.random.key(seed), 7)
    part_keys = jax.random.split(jax.random.fold_in(key_of[6], part), 7)
    velocity = centred(part_keys[0], (3, NZ + 4, NY, NX), 1.0, 5.0, ((2, 16),))
    offsets = jax.random.randint(part_keys[1], (3,), 0, DOMAIN).astype(jnp.int32)
    conv_in = centred(key_of[2], (HIDDEN_SIZE, CHANNELS, 3, 3), (9 * CHANNELS) ** -0.5, 0.625)
    conv_mid = centred(key_of[3], (HIDDEN_SIZE, HIDDEN_SIZE, 3, 3), (9 * HIDDEN_SIZE) ** -0.5, 0.25)
    conv_out = centred(key_of[4], (3 * STENCIL, HIDDEN_SIZE, 3, 3), (9 * HIDDEN_SIZE) ** -0.5, 0.25)
    cotangent = centred(part_keys[5], (3, NZ, NX, NY), 1.0, 6.0, ((2, 16),), jnp.float32)
    return {"velocity": velocity, "offsets": offsets, "conv_in": conv_in, "conv_mid": conv_mid, "conv_out": conv_out, "cotangent": cotangent}


SPREAD = 0.25
STEP_SIZE = 0.3
BASE_TAPS = (-0.0625, 0.5625, 0.5625, -0.0625)

def phase_angle(coords, offset):
    return (coords + offset).astype(jnp.float32) * (2.0 * math.pi / DOMAIN)

def positions(zcoord, ycoord, xcoord, offsets, y_first):
    angle_z = phase_angle(zcoord, offsets[2])[:, None, None]
    angle_y = phase_angle(ycoord, offsets[1])
    angle_x = phase_angle(xcoord, offsets[0])
    if y_first:
        angle_y = angle_y[None, :, None]
        angle_x = angle_x[None, None, :]
    else:
        angle_x = angle_x[None, :, None]
        angle_y = angle_y[None, None, :]
    zero_grid = jnp.zeros_like(angle_z + angle_y + angle_x)
    channel_list = [jnp.sin(angle_x), jnp.cos(angle_x), jnp.sin(angle_y), jnp.cos(angle_y), jnp.sin(angle_z), jnp.cos(angle_z)]
    return jnp.stack([item + zero_grid for item in channel_list], axis=0)

def wrap_pad(values, margin, axis_list):
    for roll_axis in axis_list:
        extent = values.shape[roll_axis]
        values = jnp.concatenate([lax.slice_in_dim(values, extent - margin, extent, axis=roll_axis), values, lax.slice_in_dim(values, 0, margin, axis=roll_axis)], axis=roll_axis)
    return values

def conv_layer(inputs, kernel):
    return lax.conv_general_dilated(inputs.astype(jnp.float32), kernel.astype(jnp.float32), (1, 1), 'VALID', dimension_numbers=('CNHW', 'OIHW', 'CNHW'), precision=lax.Precision.HIGHEST)

def interpolation(raw_output):
    grouped = raw_output.reshape((3, 3, 4) + raw_output.shape[1:])
    base_taps = jnp.array(BASE_TAPS, dtype=jnp.float32).reshape((1, 1, 4) + (1,) * (raw_output.ndim - 1))
    mixed = base_taps + SPREAD * (grouped - lax.optimization_barrier(jnp.mean(grouped, axis=2, keepdims=True)))
    return mixed.reshape(raw_output.shape).astype(jnp.bfloat16)

def network(inputs, conv_in, conv_mid, conv_out):
    first = jax.nn.gelu(conv_layer(inputs, conv_in)).astype(jnp.bfloat16)
    second = jax.nn.gelu(conv_layer(first, conv_mid)).astype(jnp.bfloat16)
    return interpolation(conv_layer(second, conv_out))

def advect(padded, weights, row_direction):
    rows = padded.shape[2] - 4
    depth = padded.shape[1] - 4
    middle = padded[:, 2:2 + depth, 2:2 + rows]
    grouped = weights.reshape((3, 3, 4) + middle.shape[1:])
    change = jnp.zeros_like(middle)
    for direction in (0, 1, 2):
        nearby = {}
        for offset in (-2, -1, 0, 1, 2):
            if direction == 2:
                nearby[offset] = padded[:, 2 + offset:2 + offset + depth, 2:2 + rows]
            elif direction == row_direction:
                nearby[offset] = padded[:, 2:2 + depth, 2 + offset:2 + offset + rows]
            else:
                nearby[offset] = jnp.roll(middle, -offset, axis=3)
        speed_up = 0.5 * (middle[direction] + nearby[1][direction])
        speed_down = 0.5 * (middle[direction] + nearby[-1][direction])
        face_up = sum((grouped[:, direction, tap_index] * nearby[tap_index - 1] for tap_index in range(4)))
        face_down = sum((grouped[:, direction, tap_index] * nearby[tap_index - 2] for tap_index in range(4)))
        change = change + speed_up * face_up - speed_down * face_down
    return middle - STEP_SIZE * change

def reference(velocity, offsets, conv_in, conv_mid, conv_out, cotangent):
    zcoord = jnp.arange(NZ, dtype=jnp.int32)
    ycoord = jnp.arange(NY, dtype=jnp.int32)
    xcoord = jnp.arange(NX, dtype=jnp.int32)
    features = positions(zcoord, ycoord, xcoord, offsets, True).astype(jnp.bfloat16)
    inputs = wrap_pad(jnp.concatenate([velocity[:, 2:2 + NZ], features], axis=0), 3, (2, 3))
    stencil = network(inputs, conv_in, conv_mid, conv_out)
    weights = jnp.swapaxes(stencil, 2, 3).astype(jnp.float32)
    start = jnp.swapaxes(velocity, 2, 3).astype(jnp.float32)
    ghost_low = start[:, :2]
    ghost_high = start[:, 2 + NZ:]

    def forward(weight_values):
        middle = advect(wrap_pad(start, 2, (2,)), weight_values, 0)
        full = jnp.concatenate([ghost_low, middle, ghost_high], axis=1)
        return advect(wrap_pad(full, 2, (2,)), weight_values, 0)
    final_state, pull = jax.vjp(forward, weights)
    gradient, = pull(cotangent)
    return (final_state, jnp.swapaxes(gradient, 2, 3).astype(jnp.bfloat16))
```

```python
import functools
import math

import jax
import jax.numpy as jnp
from jax import lax
from jax.experimental import pallas as pl
from jax.experimental.pallas import tpu as pltpu
from jax.sharding import PartitionSpec as P

DOMAIN = 1024
SPREAD = 0.25
STEP_SIZE = 0.3
BASE_TAPS = (-0.0625, 0.5625, 0.5625, -0.0625)

DEPTH = 4
ROWS = 8
SPAN = 24
HIDDEN = 64
WEIGHTS = 36
INPUT_PITCH = 33
WEIGHT_PITCH = DEPTH * SPAN + 1
PACKED = 48
F32 = jnp.float32
BF16 = jnp.bfloat16


def lane_tiles(length):
    return length // 128


def put_rows(ref, start, count, stride, values):
    for tile in range(ref.shape[0]):
        part = values[:, 128 * tile : 128 * tile + 128]
        if stride == 1:
            ref[tile, start : start + count, :] = part
        else:
            ref[tile, pl.ds(start, count, stride=stride), :] = part


def get_rows(ref, start, count):
    parts = [ref[tile, start : start + count, :] for tile in range(ref.shape[0])]
    return parts[0] if len(parts) == 1 else jnp.concatenate(parts, axis=1)


def roll_lanes(values, shift):
    width = values.shape[-1]
    shift = shift % width
    if shift == 0:
        return values
    return pltpu.roll(values, shift, values.ndim - 1)


def prepare_kernel(
    devices,
    offsets_ref,
    velocity_ref,
    cotangent_ref,
    conv_in_ref,
    conv_mid_ref,
    conv_out_ref,
    send_ref,
    own_ref,
    table_ref,
    *rest,
):
    length = velocity_ref.shape[3]
    matrices, scratch = rest[:6], rest[6:]
    for c in range(3):
        for z in range(2 * DEPTH):
            own_ref[c, z] = velocity_ref[c, z].astype(F32)
    fill_tables(offsets_ref, table_ref, ROWS * devices)
    fill_weights(conv_in_ref, conv_mid_ref, conv_out_ref, scratch, matrices[0:3], True)
    fill_weights(conv_in_ref, conv_mid_ref, conv_out_ref, scratch, matrices[3:6], False)
    interior = [velocity_ref[c, 2 + z].astype(F32) for c in range(3) for z in range(DEPTH)]
    ghosts = [velocity_ref[c, z].astype(F32) for c in range(3) for z in (0, 1, 6, 7)]
    turned = [cotangent_ref[c, z] for c in range(3) for z in range(DEPTH)]
    wide = [interior[0:4], interior[4:8], interior[8:12]]
    narrow = [ghosts[0:8], ghosts[8:12] + turned[0:4], turned[4:12]]
    groups = []
    for members in wide:
        groups.append(([roll_lanes(m, 32 * j) for j, m in enumerate(members)], 5, 32))
    for members in narrow:
        groups.append(([roll_lanes(m, 16 * j) for j, m in enumerate(members)], 2, 16))
    lane = lax.broadcasted_iota(jnp.int32, (ROWS, length), 1)

    def one(dest):
        picked = {}
        for halo, width in ((5, 32), (2, 16)):
            place = lane + (halo - ROWS * dest)
            place = jnp.where(place < 0, place + length, place)
            place = jnp.where(place >= length, place - length, place)
            picked[width] = [place < width * j for j in range(1, 128 // width)]
        done = []
        for members, halo, width in groups:
            mixed = members[-1]
            for j in range(len(members) - 2, -1, -1):
                mixed = jnp.where(picked[width][j], members[j], mixed)
            if isinstance(dest, int):
                moved = roll_lanes(mixed, halo - ROWS * dest)
            else:
                moved = pltpu.roll(mixed, (halo + length - ROWS * dest) % length, 1)
            done.append(moved[:, 0:128])
        for pair in range(3):
            both = jnp.concatenate([done[2 * pair], done[2 * pair + 1]], axis=0)
            send_ref[dest, 16 * pair : 16 * pair + 16, :] = both.astype(BF16)

    if devices <= 16:
        for dest in range(devices):
            one(dest)
    else:

        def body(dest, carry):
            one(dest)
            return carry

        lax.fori_loop(0, devices, body, 0)


def fill_weights(conv_in_ref, conv_mid_ref, conv_out_ref, scratch, matrices, rows_first):
    in_t, mid, out = scratch
    in_t[...] = jnp.zeros_like(in_t)
    for i in range(9):
        for p in range(3):
            taps = conv_in_ref[i, p].astype(F32)
            if rows_first:
                in_t[pl.ds(32 * p + i, 3, stride=9), 0:HIDDEN] = taps
            else:
                in_t[pl.ds(9 * p + i, 3, stride=32), 0:HIDDEN] = taps
    for p in range(3):
        for q in range(3):
            a, b = (p, q) if rows_first else (q, p)
            mid[HIDDEN * a : HIDDEN * a + HIDDEN, HIDDEN * b : HIDDEN * b + HIDDEN] = conv_mid_ref[p, q].astype(F32)
            out[40 * a : 40 * a + WEIGHTS, HIDDEN * b : HIDDEN * b + HIDDEN] = conv_out_ref[p, q].astype(F32)
    matrices[0][...] = in_t[...].T[0:HIDDEN].astype(BF16)
    matrices[1][...] = mid[...].astype(BF16)
    matrices[2][...] = out[...].astype(BF16)


def angle(coords, offset):
    return (coords + offset).astype(F32) * (2.0 * math.pi / DOMAIN)


def row_numbers(length, total):
    rows = lax.axis_index("gx") * ROWS - 8 + lax.broadcasted_iota(jnp.int32, (SPAN, length), 0)
    rows = jnp.where(rows < 0, rows + total, rows)
    return jnp.where(rows >= total, rows - total, rows)


def fill_tables(offsets_ref, table_ref, total):
    length = table_ref.shape[2]
    lanes = lax.broadcasted_iota(jnp.int32, (8, length), 1)
    layers = lax.broadcasted_iota(jnp.int32, (8, length), 0)
    rows = row_numbers(length, total)
    for axis in range(3):
        parts = [layers] if axis == 2 else [lanes, rows]
        coords = jnp.concatenate(parts, axis=0)
        turn = angle(coords, offsets_ref[axis])
        table_ref[2 * axis, 0 : turn.shape[0], :] = jnp.sin(turn)
        table_ref[2 * axis + 1, 0 : turn.shape[0], :] = jnp.cos(turn)


def fill_inputs(planes, u_ref, table_ref, row0, count, rows_first):
    length = u_ref.shape[3]

    def put(z, channel, q, values):
        put_rows(planes, z * count * INPUT_PITCH + 9 * q + channel, count, INPUT_PITCH, values)

    zero = jnp.zeros((DEPTH * count, length), F32)
    for spare in range(27, 32):
        put_rows(planes, spare, DEPTH * count, INPUT_PITCH, zero)
    row_axis, lane_axis = (1, 0) if rows_first else (0, 1)
    for part in range(2):
        rows = table_ref[2 * row_axis + part, 8 + row0 : 8 + row0 + count, :]
        row_of_lanes = table_ref[2 * lane_axis + part, 0:1, :]
        for z in range(DEPTH):
            layer = jnp.broadcast_to(table_ref[4 + part, z : z + 1, :], (count, length))
            for q in range(3):
                put(z, 3 + 2 * row_axis + part, q, rows)
                put(z, 7 + part, q, layer)
        for q in range(3):
            lanes = jnp.broadcast_to(roll_lanes(row_of_lanes, 1 - q), (count, length))
            for z in range(DEPTH):
                put(z, 3 + 2 * lane_axis + part, q, lanes)
    for c in range(3):
        for z in range(DEPTH):
            values = u_ref[c, 2 + z, row0 : row0 + count, :]
            for q in range(3):
                put(z, c, q, roll_lanes(values, 1 - q))


def gelu(x):
    return jax.nn.gelu(x)


def spread(values, ref, row):
    length = values.shape[1] // DEPTH
    values = values.astype(BF16)
    ref[row, HIDDEN : 2 * HIDDEN, :] = values
    for z in range(DEPTH):
        lanes = slice(z * length, (z + 1) * length)
        ref[row, 0:HIDDEN, lanes] = roll_lanes(values[:, lanes], 1)
        ref[row, 2 * HIDDEN :, lanes] = roll_lanes(values[:, lanes], -1)


def tap_sums(matrix, ref, first, last, block, part, carry, emit):
    def body(step, state):
        base = first + step * block
        older = carry[0]
        newer = carry[1]
        for j in range(block):
            product = jnp.dot(matrix, ref[base + j], preferred_element_type=F32)
            emit(base + j, older + product[2 * part : 3 * part])
            older = newer + product[part : 2 * part]
            newer = product[0:part]
        carry[0] = older
        carry[1] = newer
        return state

    lax.fori_loop(0, (last - first) // block, body, 0)


def network(planes, stacked, first_ref, second_ref, carry_mid, carry_out, matrices, raw_ref, count, blocks, row0):
    length = stacked.shape[2] // DEPTH
    for z in range(DEPTH):
        for row in range(count):
            start = (z * count + row) * INPUT_PITCH
            stacked[row, :, z * length : (z + 1) * length] = get_rows(planes, start, 32).astype(BF16)
    matrix_in = matrices[0][...]

    def first_body(step, state):
        for j in range(blocks[0]):
            row = step * blocks[0] + j
            operand = stacked[pl.ds(row, 3)].reshape(96, DEPTH * length)
            spread(gelu(jnp.dot(matrix_in, operand, preferred_element_type=F32)), first_ref, row)
        return state

    lax.fori_loop(0, (count - 2) // blocks[0], first_body, 0)
    matrix_mid = matrices[1][...]

    def emit_second(row, values):
        spread(gelu(values), second_ref, row)

    tap_sums(matrix_mid, first_ref, 0, count - 2, blocks[1], HIDDEN, carry_mid, emit_second)
    matrix_out = matrices[2][...]

    def emit_raw(row, values):
        for z in range(DEPTH):
            lanes = values[0:WEIGHTS, z * length : (z + 1) * length]
            for tile in range(lane_tiles(length)):
                raw_ref[tile, pl.ds(z * SPAN + row0 + row - 4, WEIGHTS, stride=WEIGHT_PITCH), :] = lanes[
                    :, 128 * tile : 128 * tile + 128
                ]

    tap_sums(matrix_out, second_ref, 2, count - 2, blocks[2], 40, carry_out, emit_raw)


def at(ref, k, z, row, count):
    return get_rows(ref, k * WEIGHT_PITCH + z * SPAN + row, count)


def nearby(ref, c, z, row, count, direction, row_direction, steps):
    if direction == 2:
        return {t: ref[c, 2 + z + t, row : row + count, :] for t in steps}
    if direction == row_direction:
        return {t: ref[c, 2 + z, row + t : row + t + count, :] for t in steps}
    centre = ref[c, 2 + z, row : row + count, :]
    return {t: roll_lanes(centre, -t) for t in steps}


def speeds(ref, z, row, count, direction, row_direction):
    u = nearby(ref, direction, z, row, count, direction, row_direction, (-1, 0, 1))
    return 0.5 * (u[0] + u[1]), 0.5 * (u[0] + u[-1])


def advect(u_ref, w_ref, row, count, row_direction, from_raw, emit):
    for z in range(DEPTH):
        pace = [speeds(u_ref, z, row, count, d, row_direction) for d in range(3)]
        for c in range(3):
            change = None
            for d in range(3):
                taps = [at(w_ref, 12 * c + 4 * d + s, z, row, count) for s in range(4)]
                if from_raw:
                    mean = 0.25 * ((taps[0] + taps[1]) + (taps[2] + taps[3]))
                    for s in range(4):
                        taps[s] = (BASE_TAPS[s] + SPREAD * (taps[s] - mean)).astype(BF16).astype(F32)
                        put_rows(w_ref, (12 * c + 4 * d + s) * WEIGHT_PITCH + z * SPAN + row, count, 1, taps[s])
                u = nearby(u_ref, c, z, row, count, d, row_direction, (-2, -1, 0, 1, 2))
                up = (taps[0] * u[-1] + taps[1] * u[0]) + (taps[2] * u[1] + taps[3] * u[2])
                down = (taps[0] * u[-2] + taps[1] * u[-1]) + (taps[2] * u[0] + taps[3] * u[1])
                term = pace[d][0] * up - pace[d][1] * down
                change = term if change is None else change + term
            centre = u_ref[c, 2 + z, row : row + count, :]
            emit(c, z, row, count, centre - STEP_SIZE * change)


def y_kernel(
    even_ref,
    odd_ref,
    own_hbm,
    table_hbm,
    in_hbm,
    mid_hbm,
    out_hbm,
    stencil_ref,
    start_ref,
    middle_ref,
    planes,
    stacked,
    first_ref,
    second_ref,
    carry_mid,
    carry_out,
    own_ref,
    table_ref,
    in_ref,
    mid_ref,
    out_ref,
    arrived,
):
    copies = [
        pltpu.make_async_copy(source, target, arrived.at[i])
        for i, (source, target) in enumerate(
            (
                (own_hbm, own_ref),
                (table_hbm, table_ref),
                (in_hbm, in_ref),
                (mid_hbm, mid_ref),
                (out_hbm, out_ref),
            )
        )
    ]
    for copy in copies:
        copy.start()
    is_even = lax.rem(lax.axis_index("gx"), 2) == 0
    for c in range(3):
        for z in range(2 * DEPTH):
            pair = even_ref[c, z].astype(F32)
            other = odd_ref[c, z].astype(F32)
            start_ref[c, z, 0:8, :] = jnp.where(is_even, other, pair)
            start_ref[c, z, 16:24, :] = jnp.where(is_even, pair, other)
    for copy in copies:
        copy.wait()
    for c in range(3):
        for z in range(2 * DEPTH):
            start_ref[c, z, 8:16, :] = own_ref[c, z]
    fill_inputs(planes, start_ref, table_ref, 1, 22, True)
    network(
        planes,
        stacked,
        first_ref,
        second_ref,
        carry_mid,
        carry_out,
        (in_ref, mid_ref, out_ref),
        stencil_ref,
        22,
        (5, 5, 6),
        4,
    )

    def emit(c, z, row, count, values):
        middle_ref[c, 2 + z, row : row + count, :] = values

    for row in (4, 12):
        advect(start_ref, stencil_ref, row, 8, 1, True, emit)
    for c in range(3):
        for z in (0, 1, 6, 7):
            middle_ref[c, z] = start_ref[c, z]


def adjoint_terms(u_ref, w_ref, g_ref, z, row, count, direction, put, grads):
    up_speed, down_speed = speeds(u_ref, z, row, count, direction, 1)
    into_up = None
    parts = []
    for c in range(3):
        scaled = -STEP_SIZE * g_ref[c, z, row : row + count, :]
        u = nearby(u_ref, c, z, row, count, direction, 1, (-2, -1, 0, 1, 2))
        h_up = scaled * up_speed
        h_down = scaled * down_speed
        if grads is not None:
            for s in range(4):
                grads(12 * c + 4 * direction + s, z, h_up * u[s - 1] - h_down * u[s - 2])
        if put is None:
            continue
        w = [at(w_ref, 12 * c + 4 * direction + s, z, row, count) for s in range(4)]
        up = (w[0] * u[-1] + w[1] * u[0]) + (w[2] * u[1] + w[3] * u[2])
        down = (w[0] * u[-2] + w[1] * u[-1]) + (w[2] * u[0] + w[3] * u[1])
        if into_up is None:
            into_up = scaled * up
            into_down = scaled * down
        else:
            into_up = into_up + scaled * up
            into_down = into_down + scaled * down
        parts.append(
            {
                -2: -h_down * w[0],
                -1: h_up * w[0] - h_down * w[1],
                0: h_up * w[1] - h_down * w[2],
                1: h_up * w[2] - h_down * w[3],
                2: h_up * w[3],
            }
        )
    if put is not None:
        own = parts[direction]
        own[0] = own[0] + 0.5 * (into_up - into_down)
        own[1] = own[1] + 0.5 * into_up
        own[-1] = own[-1] - 0.5 * into_down
        for c in range(3):
            put(c, parts[c])


def x_kernel(
    received_ref,
    stencil_ref,
    start_ref,
    middle_ref,
    table_ref,
    in_ref,
    mid_ref,
    out_ref,
    final_ref,
    grads_ref,
    planes,
    stacked,
    first_ref,
    second_ref,
    carry_mid,
    carry_out,
    own_ref,
    turned_ref,
    back_ref,
    raw_ref,
    next_ref,
):
    length = start_ref.shape[3]

    def group(g):
        half = received_ref[:, 16 * (g // 2) : 16 * (g // 2) + 16, :].astype(F32)
        half = half[:, 8 * (g % 2) : 8 * (g % 2) + 8, :]
        return half.reshape(length, 128).T

    for g in range(3):
        block = group(g)
        for j in range(4):
            own_ref[g, 2 + j, 3:21, :] = block[32 * j : 32 * j + 18]
    ghost_layers = [(c, z) for c in range(3) for z in (0, 1, 6, 7)]
    inner_layers = [(c, z) for c in range(3) for z in range(DEPTH)]
    narrow = [(own_ref,) + layer for layer in ghost_layers] + [(turned_ref,) + layer for layer in inner_layers]
    for g in range(3):
        block = group(3 + g)
        for j in range(8):
            ref, c, z = narrow[8 * g + j]
            ref[c, z, 6:18, :] = block[16 * j : 16 * j + 12]

    for c in range(3):
        for z in range(DEPTH):
            back_ref[c, z, 8:16, :] = turned_ref[c, z, 8:16, :]

    def keep(k, z, values):
        put_rows(raw_ref, k * WEIGHT_PITCH + z * SPAN, ROWS, 1, values)

    for direction in range(3):
        blocks = ((8, 8, keep), (6, 2, None), (16, 2, None)) if direction == 1 else ((8, 8, keep),)
        for row, count, grads in blocks:
            for z in range(DEPTH):

                def put(c, parts):
                    if direction == 0:
                        total_part = parts[0]
                        for t in (-2, -1, 1, 2):
                            total_part = total_part + roll_lanes(parts[t], t)
                        back_ref[c, z, 8:16, :] += total_part
                    elif direction == 2:
                        for t in (-2, -1, 0, 1, 2):
                            if 0 <= z + t < DEPTH:
                                back_ref[c, z + t, 8:16, :] += parts[t]
                    else:
                        for t in (-2, -1, 0, 1, 2):
                            back_ref[c, z, row + t : row + t + count, :] += parts[t]

                adjoint_terms(middle_ref, stencil_ref, turned_ref, z, row, count, direction, put, grads)

    def finish(k, z, values):
        later = get_rows(raw_ref, k * WEIGHT_PITCH + z * SPAN, ROWS)
        grads_ref[k, z] = (later + values).astype(BF16)

    for direction in range(3):
        for z in range(DEPTH):
            adjoint_terms(start_ref, stencil_ref, back_ref, z, 8, 8, direction, None, finish)

    fill_inputs(planes, own_ref, table_ref, 3, 18, False)
    network(
        planes,
        stacked,
        first_ref,
        second_ref,
        carry_mid,
        carry_out,
        (in_ref, mid_ref, out_ref),
        raw_ref,
        18,
        (4, 4, 7),
        6,
    )

    def emit_middle(c, z, row, count, values):
        next_ref[c, 2 + z, row : row + count, :] = values

    for row, count in ((6, 8), (14, 4)):
        advect(own_ref, raw_ref, row, count, 0, True, emit_middle)
    for c, z in ghost_layers:
        next_ref[c, z, 8:16, :] = own_ref[c, z, 8:16, :]

    def emit_final(c, z, row, count, values):
        final_ref[c, z] = values

    advect(next_ref, raw_ref, 8, 8, 0, False, emit_final)


def network_scratch(count, length):
    lanes = DEPTH * length
    return [
        pltpu.VMEM((lane_tiles(length), DEPTH * count * INPUT_PITCH, 128), F32),
        pltpu.VMEM((count, 32, lanes), BF16),
        pltpu.VMEM((count - 2, 3 * HIDDEN, lanes), BF16),
        pltpu.VMEM((count - 2, 3 * HIDDEN, lanes), BF16),
        pltpu.VMEM((2, HIDDEN, lanes), F32),
        pltpu.VMEM((2, 40, lanes), F32),
    ]


def on_device(velocity, offsets, conv_in, conv_mid, conv_out, cotangent):
    devices = lax.axis_size("gx")
    length = velocity.shape[3]
    assert velocity.shape[2] == ROWS and velocity.shape[1] == 2 * DEPTH and length == ROWS * devices
    pairs = [(i, i ^ 1) for i in range(devices)]
    others = [(i, (i + 1) % devices if i % 2 else (i - 1) % devices) for i in range(devices)]
    odd = lax.ppermute(velocity, "gx", others)
    even = lax.ppermute(velocity, "gx", pairs)
    vmem = pl.BlockSpec(memory_space=pltpu.VMEM)
    smem = pl.BlockSpec(memory_space=pltpu.SMEM)
    hbm = pl.BlockSpec(memory_space=pltpu.HBM)
    in_taps = jnp.transpose(conv_in, (1, 2, 3, 0))
    mid_taps = jnp.transpose(conv_mid, (2, 3, 0, 1))
    out_taps = jnp.transpose(conv_out, (2, 3, 0, 1))
    slab = (3, 2 * DEPTH, SPAN, length)
    weights = (lane_tiles(length), WEIGHTS * WEIGHT_PITCH, 128)
    shapes = (
        ((devices, PACKED, 128), BF16),
        ((3, 2 * DEPTH, ROWS, length), F32),
        ((6, 8 + SPAN, length), F32),
    ) + (((HIDDEN, 96), BF16), ((3 * HIDDEN, 3 * HIDDEN), BF16), ((120, 3 * HIDDEN), BF16)) * 2
    prepared = pl.pallas_call(
        functools.partial(prepare_kernel, devices),
        out_shape=tuple(jax.ShapeDtypeStruct(*shape) for shape in shapes),
        in_specs=[smem] + [vmem] * 5,
        out_specs=(vmem,) * len(shapes),
        scratch_shapes=[
            pltpu.VMEM((96, 128), F32),
            pltpu.VMEM((3 * HIDDEN, 3 * HIDDEN), F32),
            pltpu.VMEM((120, 3 * HIDDEN), F32),
        ],
        name="prepare",
    )(offsets, velocity, cotangent, in_taps, mid_taps, out_taps)
    send, own, table = prepared[:3]
    received = lax.all_to_all(send, "gx", 0, 0)
    limit = pltpu.CompilerParams(vmem_limit_bytes=(40 if length <= 128 else 60) << 20)
    stencil, start, middle = pl.pallas_call(
        y_kernel,
        out_shape=(
            jax.ShapeDtypeStruct(weights, F32),
            jax.ShapeDtypeStruct(slab, F32),
            jax.ShapeDtypeStruct(slab, F32),
        ),
        in_specs=[vmem] * 2 + [hbm] * 5,
        out_specs=(vmem, vmem, vmem),
        scratch_shapes=network_scratch(22, length)
        + [pltpu.VMEM(*shape) for shape in shapes[1:6]]
        + [pltpu.SemaphoreType.DMA((5,))],
        compiler_params=limit,
        cost_estimate=pl.CostEstimate(flops=4 * 10**9, transcendentals=10**6, bytes_accessed=10**7),
        name="y_slab",
    )(even, odd, own, table, *prepared[3:6])
    final_state, weight_grads = pl.pallas_call(
        x_kernel,
        out_shape=(
            jax.ShapeDtypeStruct((3, DEPTH, ROWS, length), F32),
            jax.ShapeDtypeStruct((WEIGHTS, DEPTH, ROWS, length), BF16),
        ),
        in_specs=[vmem] * 8,
        out_specs=(vmem, vmem),
        scratch_shapes=network_scratch(18, length)
        + [
            pltpu.VMEM(slab, F32),
            pltpu.VMEM((3, DEPTH, SPAN, length), F32),
            pltpu.VMEM((3, DEPTH, SPAN, length), F32),
            pltpu.VMEM(weights, F32),
            pltpu.VMEM(slab, F32),
        ],
        compiler_params=limit,
        cost_estimate=pl.CostEstimate(flops=3 * 10**9, transcendentals=10**6, bytes_accessed=10**7),
        name="x_slab",
    )(received, stencil, start, middle, table, *prepared[6:9])
    return (final_state, weight_grads)


def solution(mesh):
    return jax.shard_map(
        on_device,
        mesh=mesh,
        in_specs=(
            P(None, "groups", "gx", None),
            P("groups"),
            P(),
            P(),
            P(),
            P(None, "groups", "gx", None),
        ),
        out_specs=(P(None, "groups", "gx", None), P(None, "groups", "gx", None)),
        check_vma=False,
    )
```

```python
import functools
import math

import jax
import jax.numpy as jnp
from jax import lax
from jax.experimental import pallas as pl
from jax.experimental.pallas import tpu as pltpu
from jax.sharding import PartitionSpec as P

DOMAIN = 1024
SPREAD = 0.25
STEP_SIZE = 0.3
BASE_TAPS = (-0.0625, 0.5625, 0.5625, -0.0625)

DEPTH = 4
ROWS = 8
SPAN = 24
HIDDEN = 64
WEIGHTS = 36
INPUT_PITCH = 33
WEIGHT_PITCH = DEPTH * SPAN + 1
PACKED = 32
F32 = jnp.float32
BF16 = jnp.bfloat16


def lane_tiles(length):
    return length // 128


def put_rows(ref, start, count, stride, values):
    for tile in range(ref.shape[0]):
        part = values[:, 128 * tile : 128 * tile + 128]
        if stride == 1:
            ref[tile, start : start + count, :] = part
        else:
            ref[tile, pl.ds(start, count, stride=stride), :] = part


def get_rows(ref, start, count):
    parts = [ref[tile, start : start + count, :] for tile in range(ref.shape[0])]
    return parts[0] if len(parts) == 1 else jnp.concatenate(parts, axis=1)


def roll_lanes(values, shift):
    width = values.shape[-1]
    shift = shift % width
    if shift == 0:
        return values
    return pltpu.roll(values, shift, values.ndim - 1)


def message_places():
    places = [[(p, 18 * p, 18, 0) for p in range(7)]]
    places.append([(7 + p, 18 * p, 18, 0) for p in range(5)] + [(12 + p, 90 + 12 * p, 12, 0) for p in range(3)])
    places.append([(15 + p, 12 * p, 12, 0) for p in range(10)] + [(35, 120, 8, 0)])
    places.append([(25 + p, 12 * p, 12, 0) for p in range(10)] + [(35, 120, 4, 8)])
    return places


def prepare_kernel(
    devices,
    offsets_ref,
    velocity_ref,
    cotangent_ref,
    conv_in_ref,
    conv_mid_ref,
    conv_out_ref,
    send_ref,
    own_ref,
    table_ref,
    *rest,
):
    length = velocity_ref.shape[3]
    matrices, scratch = rest[:6], rest[6:]
    for c in range(3):
        for z in range(2 * DEPTH):
            own_ref[c, z] = velocity_ref[c, z].astype(F32)
    fill_tables(offsets_ref, table_ref, ROWS * devices)
    fill_weights(conv_in_ref, conv_mid_ref, conv_out_ref, scratch, matrices[0:3], True)
    fill_weights(conv_in_ref, conv_mid_ref, conv_out_ref, scratch, matrices[3:6], False)
    planes = [velocity_ref[c, 2 + z].astype(F32) for c in range(3) for z in range(DEPTH)]
    planes += [velocity_ref[c, z].astype(F32) for c in range(3) for z in (0, 1, 6, 7)]
    planes += [cotangent_ref[c, z] for c in range(3) for z in range(DEPTH)]
    groups = []
    for places in message_places():
        members = []
        for plane, first, lanes, skipped in places:
            halo = 5 if plane < 12 else 2
            members.append((roll_lanes(planes[plane], first - skipped + halo), first))
        groups.append(members)
    lane = lax.broadcasted_iota(jnp.int32, (ROWS, length), 1)

    def one(dest):
        place = lane - ROWS * dest
        place = jnp.where(place < 0, place + length, place)
        done = []
        for members in groups:
            mixed = members[0][0]
            for values, first in members[1:]:
                mixed = jnp.where(place < first, mixed, values)
            if isinstance(dest, int):
                moved = roll_lanes(mixed, -ROWS * dest)
            else:
                moved = pltpu.roll(mixed, length - ROWS * dest, 1)
            done.append(moved[:, 0:128])
        for pair in range(2):
            both = jnp.concatenate([done[2 * pair], done[2 * pair + 1]], axis=0)
            send_ref[dest, 16 * pair : 16 * pair + 16, :] = both.astype(BF16)

    if devices <= 16:
        for dest in range(devices):
            one(dest)
    else:

        def body(dest, carry):
            one(dest)
            return carry

        lax.fori_loop(0, devices, body, 0)


def fill_weights(conv_in_ref, conv_mid_ref, conv_out_ref, scratch, matrices, rows_first):
    in_t, mid, out = scratch
    in_t[...] = jnp.zeros_like(in_t)
    for i in range(9):
        for p in range(3):
            taps = conv_in_ref[i, p].astype(F32)
            if rows_first:
                in_t[pl.ds(32 * p + i, 3, stride=9), 0:HIDDEN] = taps
            else:
                in_t[pl.ds(9 * p + i, 3, stride=32), 0:HIDDEN] = taps
    for p in range(3):
        for q in range(3):
            a, b = (p, q) if rows_first else (q, p)
            mid[HIDDEN * a : HIDDEN * a + HIDDEN, HIDDEN * b : HIDDEN * b + HIDDEN] = conv_mid_ref[p, q].astype(F32)
            out[40 * a : 40 * a + WEIGHTS, HIDDEN * b : HIDDEN * b + HIDDEN] = conv_out_ref[p, q].astype(F32)
    matrices[0][...] = in_t[...].T[0:HIDDEN].astype(BF16)
    matrices[1][...] = mid[...].astype(BF16)
    matrices[2][...] = out[...].astype(BF16)


def angle(coords, offset):
    return (coords + offset).astype(F32) * (2.0 * math.pi / DOMAIN)


def row_numbers(length, total):
    rows = lax.axis_index("gx") * ROWS - 8 + lax.broadcasted_iota(jnp.int32, (SPAN, length), 0)
    rows = jnp.where(rows < 0, rows + total, rows)
    return jnp.where(rows >= total, rows - total, rows)


def fill_tables(offsets_ref, table_ref, total):
    length = table_ref.shape[2]
    lanes = lax.broadcasted_iota(jnp.int32, (8, length), 1)
    layers = lax.broadcasted_iota(jnp.int32, (8, length), 0)
    rows = row_numbers(length, total)
    for axis in range(3):
        parts = [layers] if axis == 2 else [lanes, rows]
        coords = jnp.concatenate(parts, axis=0)
        turn = angle(coords, offsets_ref[axis])
        table_ref[2 * axis, 0 : turn.shape[0], :] = jnp.sin(turn)
        table_ref[2 * axis + 1, 0 : turn.shape[0], :] = jnp.cos(turn)


def fill_inputs(planes, u_ref, table_ref, row0, count, rows_first):
    length = u_ref.shape[3]

    def put(z, channel, q, values):
        put_rows(planes, z * count * INPUT_PITCH + 9 * q + channel, count, INPUT_PITCH, values)

    zero = jnp.zeros((DEPTH * count, length), F32)
    for spare in range(27, 32):
        put_rows(planes, spare, DEPTH * count, INPUT_PITCH, zero)
    row_axis, lane_axis = (1, 0) if rows_first else (0, 1)
    for part in range(2):
        rows = table_ref[2 * row_axis + part, 8 + row0 : 8 + row0 + count, :]
        row_of_lanes = table_ref[2 * lane_axis + part, 0:1, :]
        for z in range(DEPTH):
            layer = jnp.broadcast_to(table_ref[4 + part, z : z + 1, :], (count, length))
            for q in range(3):
                put(z, 3 + 2 * row_axis + part, q, rows)
                put(z, 7 + part, q, layer)
        for q in range(3):
            lanes = jnp.broadcast_to(roll_lanes(row_of_lanes, 1 - q), (count, length))
            for z in range(DEPTH):
                put(z, 3 + 2 * lane_axis + part, q, lanes)
    for c in range(3):
        for z in range(DEPTH):
            values = u_ref[c, 2 + z, row0 : row0 + count, :]
            for q in range(3):
                put(z, c, q, roll_lanes(values, 1 - q))


def gelu(x):
    return jax.nn.gelu(x)


def spread(values, ref, row):
    length = values.shape[1] // DEPTH
    values = values.astype(BF16)
    ref[row, HIDDEN : 2 * HIDDEN, :] = values
    for z in range(DEPTH):
        lanes = slice(z * length, (z + 1) * length)
        ref[row, 0:HIDDEN, lanes] = roll_lanes(values[:, lanes], 1)
        ref[row, 2 * HIDDEN :, lanes] = roll_lanes(values[:, lanes], -1)


def tap_sums(matrix, ref, first, last, block, part, carry, emit):
    def body(step, state):
        base = first + step * block
        older = carry[0]
        newer = carry[1]
        for j in range(block):
            product = jnp.dot(matrix, ref[base + j], preferred_element_type=F32)
            emit(base + j, older + product[2 * part : 3 * part])
            older = newer + product[part : 2 * part]
            newer = product[0:part]
        carry[0] = older
        carry[1] = newer
        return state

    lax.fori_loop(0, (last - first) // block, body, 0)


def network(planes, stacked, first_ref, second_ref, carry_mid, carry_out, matrices, raw_ref, count, blocks, row0):
    length = stacked.shape[2] // DEPTH
    for z in range(DEPTH):
        for row in range(count):
            start = (z * count + row) * INPUT_PITCH
            stacked[row, :, z * length : (z + 1) * length] = get_rows(planes, start, 32).astype(BF16)
    matrix_in = matrices[0][...]

    def first_body(step, state):
        for j in range(blocks[0]):
            row = step * blocks[0] + j
            operand = stacked[pl.ds(row, 3)].reshape(96, DEPTH * length)
            spread(gelu(jnp.dot(matrix_in, operand, preferred_element_type=F32)), first_ref, row)
        return state

    lax.fori_loop(0, (count - 2) // blocks[0], first_body, 0)
    matrix_mid = matrices[1][...]

    def emit_second(row, values):
        spread(gelu(values), second_ref, row)

    tap_sums(matrix_mid, first_ref, 0, count - 2, blocks[1], HIDDEN, carry_mid, emit_second)
    matrix_out = matrices[2][...]

    def emit_raw(row, values):
        for z in range(DEPTH):
            lanes = values[0:WEIGHTS, z * length : (z + 1) * length]
            for tile in range(lane_tiles(length)):
                raw_ref[tile, pl.ds(z * SPAN + row0 + row - 4, WEIGHTS, stride=WEIGHT_PITCH), :] = lanes[
                    :, 128 * tile : 128 * tile + 128
                ]

    tap_sums(matrix_out, second_ref, 2, count - 2, blocks[2], 40, carry_out, emit_raw)


def at(ref, k, z, row, count):
    return get_rows(ref, k * WEIGHT_PITCH + z * SPAN + row, count)


def nearby(ref, c, z, row, count, direction, row_direction, steps):
    if direction == 2:
        return {t: ref[c, 2 + z + t, row : row + count, :] for t in steps}
    if direction == row_direction:
        return {t: ref[c, 2 + z, row + t : row + t + count, :] for t in steps}
    centre = ref[c, 2 + z, row : row + count, :]
    return {t: roll_lanes(centre, -t) for t in steps}


def speeds(ref, z, row, count, direction, row_direction):
    u = nearby(ref, direction, z, row, count, direction, row_direction, (-1, 0, 1))
    return 0.5 * (u[0] + u[1]), 0.5 * (u[0] + u[-1])


def advect(u_ref, w_ref, row, count, row_direction, from_raw, emit):
    for z in range(DEPTH):
        pace = [speeds(u_ref, z, row, count, d, row_direction) for d in range(3)]
        for c in range(3):
            change = None
            for d in range(3):
                taps = [at(w_ref, 12 * c + 4 * d + s, z, row, count) for s in range(4)]
                if from_raw:
                    mean = 0.25 * ((taps[0] + taps[1]) + (taps[2] + taps[3]))
                    for s in range(4):
                        taps[s] = (BASE_TAPS[s] + SPREAD * (taps[s] - mean)).astype(BF16).astype(F32)
                        put_rows(w_ref, (12 * c + 4 * d + s) * WEIGHT_PITCH + z * SPAN + row, count, 1, taps[s])
                u = nearby(u_ref, c, z, row, count, d, row_direction, (-2, -1, 0, 1, 2))
                up = (taps[0] * u[-1] + taps[1] * u[0]) + (taps[2] * u[1] + taps[3] * u[2])
                down = (taps[0] * u[-2] + taps[1] * u[-1]) + (taps[2] * u[0] + taps[3] * u[1])
                term = pace[d][0] * up - pace[d][1] * down
                change = term if change is None else change + term
            centre = u_ref[c, 2 + z, row : row + count, :]
            emit(c, z, row, count, centre - STEP_SIZE * change)


def y_kernel(
    even_ref,
    odd_ref,
    own_ref,
    table_ref,
    in_ref,
    mid_ref,
    out_ref,
    stencil_ref,
    start_ref,
    middle_ref,
    planes,
    stacked,
    first_ref,
    second_ref,
    carry_mid,
    carry_out,
):
    is_even = lax.rem(lax.axis_index("gx"), 2) == 0
    for c in range(3):
        for z in range(2 * DEPTH):
            pair = even_ref[c, z].astype(F32)
            other = odd_ref[c, z].astype(F32)
            start_ref[c, z, 0:8, :] = jnp.where(is_even, other, pair)
            start_ref[c, z, 16:24, :] = jnp.where(is_even, pair, other)
    for c in range(3):
        for z in range(2 * DEPTH):
            start_ref[c, z, 8:16, :] = own_ref[c, z]
    fill_inputs(planes, start_ref, table_ref, 1, 22, True)
    network(
        planes,
        stacked,
        first_ref,
        second_ref,
        carry_mid,
        carry_out,
        (in_ref, mid_ref, out_ref),
        stencil_ref,
        22,
        (5, 5, 6),
        4,
    )

    def emit(c, z, row, count, values):
        middle_ref[c, 2 + z, row : row + count, :] = values

    for row in (4, 12):
        advect(start_ref, stencil_ref, row, 8, 1, True, emit)
    for c in range(3):
        for z in (0, 1, 6, 7):
            middle_ref[c, z] = start_ref[c, z]


def adjoint_terms(u_ref, w_ref, g_ref, z, row, count, direction, put, grads):
    up_speed, down_speed = speeds(u_ref, z, row, count, direction, 1)
    into_up = None
    parts = []
    for c in range(3):
        scaled = -STEP_SIZE * g_ref[c, z, row : row + count, :]
        u = nearby(u_ref, c, z, row, count, direction, 1, (-2, -1, 0, 1, 2))
        h_up = scaled * up_speed
        h_down = scaled * down_speed
        if grads is not None:
            for s in range(4):
                grads(12 * c + 4 * direction + s, z, h_up * u[s - 1] - h_down * u[s - 2])
        if put is None:
            continue
        w = [at(w_ref, 12 * c + 4 * direction + s, z, row, count) for s in range(4)]
        up = (w[0] * u[-1] + w[1] * u[0]) + (w[2] * u[1] + w[3] * u[2])
        down = (w[0] * u[-2] + w[1] * u[-1]) + (w[2] * u[0] + w[3] * u[1])
        if into_up is None:
            into_up = scaled * up
            into_down = scaled * down
        else:
            into_up = into_up + scaled * up
            into_down = into_down + scaled * down
        parts.append(
            {
                -2: -h_down * w[0],
                -1: h_up * w[0] - h_down * w[1],
                0: h_up * w[1] - h_down * w[2],
                1: h_up * w[2] - h_down * w[3],
                2: h_up * w[3],
            }
        )
    if put is not None:
        own = parts[direction]
        own[0] = own[0] + 0.5 * (into_up - into_down)
        own[1] = own[1] + 0.5 * into_up
        own[-1] = own[-1] - 0.5 * into_down
        for c in range(3):
            put(c, parts[c])


def x_kernel(
    received_ref,
    stencil_ref,
    start_ref,
    middle_ref,
    table_ref,
    in_ref,
    mid_ref,
    out_ref,
    final_ref,
    grads_ref,
    planes,
    stacked,
    first_ref,
    second_ref,
    carry_mid,
    carry_out,
    own_ref,
    turned_ref,
    back_ref,
    raw_ref,
    next_ref,
    block_ref,
):
    length = start_ref.shape[3]

    def group(g):
        half = received_ref[:, 16 * (g // 2) : 16 * (g // 2) + 16, :].astype(F32)
        half = half[:, 8 * (g % 2) : 8 * (g % 2) + 8, :]
        return half.reshape(length, 128).T

    ghost_layers = [(c, z) for c in range(3) for z in (0, 1, 6, 7)]
    targets = [(own_ref, c, 2 + z, 3) for c in range(3) for z in range(DEPTH)]
    targets += [(own_ref, c, z, 6) for c, z in ghost_layers]
    targets += [(turned_ref, c, z, 6) for c in range(3) for z in range(DEPTH)]
    for g, places in enumerate(message_places()):
        block_ref[...] = group(g)
        for plane, first, lanes, skipped in places:
            ref, c, z, row = targets[plane]
            ref[c, z, row + skipped : row + skipped + lanes, :] = block_ref[first : first + lanes, :]

    for c in range(3):
        for z in range(DEPTH):
            back_ref[c, z, 8:16, :] = turned_ref[c, z, 8:16, :]

    def keep(k, z, values):
        put_rows(raw_ref, k * WEIGHT_PITCH + z * SPAN, ROWS, 1, values)

    for direction in range(3):
        blocks = ((8, 8, keep), (6, 2, None), (16, 2, None)) if direction == 1 else ((8, 8, keep),)
        for row, count, grads in blocks:
            for z in range(DEPTH):

                def put(c, parts):
                    if direction == 0:
                        total_part = parts[0]
                        for t in (-2, -1, 1, 2):
                            total_part = total_part + roll_lanes(parts[t], t)
                        back_ref[c, z, 8:16, :] += total_part
                    elif direction == 2:
                        for t in (-2, -1, 0, 1, 2):
                            if 0 <= z + t < DEPTH:
                                back_ref[c, z + t, 8:16, :] += parts[t]
                    else:
                        for t in (-2, -1, 0, 1, 2):
                            back_ref[c, z, row + t : row + t + count, :] += parts[t]

                adjoint_terms(middle_ref, stencil_ref, turned_ref, z, row, count, direction, put, grads)

    def finish(k, z, values):
        later = get_rows(raw_ref, k * WEIGHT_PITCH + z * SPAN, ROWS)
        grads_ref[k, z] = (later + values).astype(BF16)

    for direction in range(3):
        for z in range(DEPTH):
            adjoint_terms(start_ref, stencil_ref, back_ref, z, 8, 8, direction, None, finish)

    fill_inputs(planes, own_ref, table_ref, 3, 18, False)
    network(
        planes,
        stacked,
        first_ref,
        second_ref,
        carry_mid,
        carry_out,
        (in_ref, mid_ref, out_ref),
        raw_ref,
        18,
        (4, 4, 7),
        6,
    )

    def emit_middle(c, z, row, count, values):
        next_ref[c, 2 + z, row : row + count, :] = values

    for row, count in ((6, 8), (14, 4)):
        advect(own_ref, raw_ref, row, count, 0, True, emit_middle)
    for c, z in ghost_layers:
        next_ref[c, z, 8:16, :] = own_ref[c, z, 8:16, :]

    def emit_final(c, z, row, count, values):
        final_ref[c, z] = values

    advect(next_ref, raw_ref, 8, 8, 0, False, emit_final)


def network_scratch(count, length):
    lanes = DEPTH * length
    return [
        pltpu.VMEM((lane_tiles(length), DEPTH * count * INPUT_PITCH, 128), F32),
        pltpu.VMEM((count, 32, lanes), BF16),
        pltpu.VMEM((count - 2, 3 * HIDDEN, lanes), BF16),
        pltpu.VMEM((count - 2, 3 * HIDDEN, lanes), BF16),
        pltpu.VMEM((2, HIDDEN, lanes), F32),
        pltpu.VMEM((2, 40, lanes), F32),
    ]


def on_device(velocity, offsets, conv_in, conv_mid, conv_out, cotangent):
    devices = lax.axis_size("gx")
    length = velocity.shape[3]
    assert velocity.shape[2] == ROWS and velocity.shape[1] == 2 * DEPTH and length == ROWS * devices
    pairs = [(i, i ^ 1) for i in range(devices)]
    others = [(i, (i + 1) % devices if i % 2 else (i - 1) % devices) for i in range(devices)]
    odd = lax.ppermute(velocity, "gx", others)
    even = lax.ppermute(velocity, "gx", pairs)
    vmem = pl.BlockSpec(memory_space=pltpu.VMEM)
    smem = pl.BlockSpec(memory_space=pltpu.SMEM)
    in_taps = jnp.transpose(conv_in, (1, 2, 3, 0))
    mid_taps = jnp.transpose(conv_mid, (2, 3, 0, 1))
    out_taps = jnp.transpose(conv_out, (2, 3, 0, 1))
    slab = (3, 2 * DEPTH, SPAN, length)
    weights = (lane_tiles(length), WEIGHTS * WEIGHT_PITCH, 128)
    shapes = (
        ((devices, PACKED, 128), BF16),
        ((3, 2 * DEPTH, ROWS, length), F32),
        ((6, 8 + SPAN, length), F32),
    ) + (((HIDDEN, 96), BF16), ((3 * HIDDEN, 3 * HIDDEN), BF16), ((120, 3 * HIDDEN), BF16)) * 2
    arguments = (offsets, velocity, cotangent, in_taps, mid_taps, out_taps)
    prepared = pl.pallas_call(
        functools.partial(prepare_kernel, devices),
        out_shape=tuple(jax.ShapeDtypeStruct(*shape) for shape in shapes),
        in_specs=[smem] + [vmem] * 5,
        out_specs=(vmem,) * len(shapes),
        scratch_shapes=[
            pltpu.VMEM((96, 128), F32),
            pltpu.VMEM((3 * HIDDEN, 3 * HIDDEN), F32),
            pltpu.VMEM((120, 3 * HIDDEN), F32),
        ],
        compiler_params=pltpu.CompilerParams(vmem_limit_bytes=24 << 20),
        name="prepare",
    )(*[pltpu.with_memory_space_constraint(a, pltpu.HBM) for a in arguments])
    send, own, table = prepared[:3]
    received = lax.all_to_all(send, "gx", 0, 0)
    limit = pltpu.CompilerParams(vmem_limit_bytes=(24 if length <= 128 else 61) << 20)
    stencil, start, middle = pl.pallas_call(
        y_kernel,
        out_shape=(
            jax.ShapeDtypeStruct(weights, F32),
            jax.ShapeDtypeStruct(slab, F32),
            jax.ShapeDtypeStruct(slab, F32),
        ),
        in_specs=[vmem] * 7,
        out_specs=(vmem, vmem, vmem),
        scratch_shapes=network_scratch(22, length),
        compiler_params=limit,
        cost_estimate=pl.CostEstimate(flops=4 * 10**9, transcendentals=10**6, bytes_accessed=10**7),
        name="y_slab",
    )(even, odd, own, table, *prepared[3:6])
    final_state, weight_grads = pl.pallas_call(
        x_kernel,
        out_shape=(
            jax.ShapeDtypeStruct((3, DEPTH, ROWS, length), F32),
            jax.ShapeDtypeStruct((WEIGHTS, DEPTH, ROWS, length), BF16),
        ),
        in_specs=[vmem] * 8,
        out_specs=(vmem, vmem),
        scratch_shapes=network_scratch(18, length)
        + [
            pltpu.VMEM(slab, F32),
            pltpu.VMEM((3, DEPTH, SPAN, length), F32),
            pltpu.VMEM((3, DEPTH, SPAN, length), F32),
            pltpu.VMEM(weights, F32),
            pltpu.VMEM(slab, F32),
            pltpu.VMEM((128, length), F32),
        ],
        compiler_params=limit,
        cost_estimate=pl.CostEstimate(flops=3 * 10**9, transcendentals=10**6, bytes_accessed=10**7),
        name="x_slab",
    )(received, stencil, start, middle, table, *prepared[6:9])
    return (final_state, weight_grads)


def solution(mesh):
    return jax.shard_map(
        on_device,
        mesh=mesh,
        in_specs=(
            P(None, "groups", "gx", None),
            P("groups"),
            P(),
            P(),
            P(),
            P(None, "groups", "gx", None),
        ),
        out_specs=(P(None, "groups", "gx", None), P(None, "groups", "gx", None)),
        check_vma=False,
    )
```

```python
import functools
import math

import jax
import jax.numpy as jnp
from jax import lax
from jax.experimental import pallas as pl
from jax.experimental.pallas import tpu as pltpu
from jax.sharding import PartitionSpec as P

DOMAIN = 1024
SPREAD = 0.25
STEP_SIZE = 0.3
BASE_TAPS = (-0.0625, 0.5625, 0.5625, -0.0625)

GELU_LINEAR = math.sqrt(2.0 / math.pi)
GELU_CUBIC = 0.044715 * GELU_LINEAR

DEPTH = 4
ROWS = 8
SPAN = 24
HIDDEN = 64
WEIGHTS = 36
INPUT_PITCH = 33
LAGS = (20, 40)
WEIGHT_PITCH = DEPTH * SPAN + 1
PACKED = 32
F32 = jnp.float32
BF16 = jnp.bfloat16


def lane_tiles(length):
    return length // 128


def put_rows(ref, start, count, stride, values):
    for tile in range(ref.shape[0]):
        part = values[:, 128 * tile : 128 * tile + 128]
        if stride == 1:
            ref[tile, start : start + count, :] = part
        else:
            ref[tile, pl.ds(start, count, stride=stride), :] = part


def get_rows(ref, start, count):
    parts = [ref[tile, start : start + count, :] for tile in range(ref.shape[0])]
    return parts[0] if len(parts) == 1 else jnp.concatenate(parts, axis=1)


def roll_lanes(values, shift):
    width = values.shape[-1]
    shift = shift % width
    if shift == 0:
        return values
    return pltpu.roll(values, shift, values.ndim - 1)


def message_places():
    places = [[(p, 18 * p, 18, 0) for p in range(7)]]
    places.append([(7 + p, 18 * p, 18, 0) for p in range(5)] + [(12 + p, 90 + 12 * p, 12, 0) for p in range(3)])
    places.append([(15 + p, 12 * p, 12, 0) for p in range(10)] + [(35, 120, 8, 0)])
    places.append([(25 + p, 12 * p, 12, 0) for p in range(10)] + [(35, 120, 4, 8)])
    return places


def pack_kernel(devices, velocity_ref, cotangent_ref, send_ref):
    length = velocity_ref.shape[3]
    planes = [velocity_ref[c, 2 + z].astype(F32) for c in range(3) for z in range(DEPTH)]
    planes += [velocity_ref[c, z].astype(F32) for c in range(3) for z in (0, 1, 6, 7)]
    planes += [cotangent_ref[c, z] for c in range(3) for z in range(DEPTH)]
    groups = []
    for places in message_places():
        members = []
        for plane, first, lanes, skipped in places:
            halo = 5 if plane < 12 else 2
            members.append((roll_lanes(planes[plane], first - skipped + halo), first))
        groups.append(members)
    lane = lax.broadcasted_iota(jnp.int32, (ROWS, length), 1)

    def one(dest):
        place = lane - ROWS * dest
        place = jnp.where(place < 0, place + length, place)
        done = []
        for members in groups:
            mixed = members[0][0]
            for values, first in members[1:]:
                mixed = jnp.where(place < first, mixed, values)
            if isinstance(dest, int):
                moved = roll_lanes(mixed, -ROWS * dest)
            else:
                moved = pltpu.roll(mixed, length - ROWS * dest, 1)
            done.append(moved[:, 0:128])
        for pair in range(2):
            both = jnp.concatenate([done[2 * pair], done[2 * pair + 1]], axis=0)
            send_ref[dest, 16 * pair : 16 * pair + 16, :] = both.astype(BF16)

    if devices <= 16:
        for dest in range(devices):
            one(dest)
    else:

        def body(dest, carry):
            one(dest)
            return carry

        lax.fori_loop(0, devices, body, 0)


def fill_weights(conv_in_ref, conv_mid_ref, conv_out_ref, scratch, matrices, rows_first):
    in_t, mid, out = scratch
    in_t[...] = jnp.zeros_like(in_t)
    for i in range(9):
        for p in range(3):
            taps = conv_in_ref[i, p].astype(F32)
            if rows_first:
                in_t[pl.ds(32 * p + i, 3, stride=9), 0:HIDDEN] = taps
            else:
                in_t[pl.ds(9 * p + i, 3, stride=32), 0:HIDDEN] = taps
    for p in range(3):
        for q in range(3):
            a, b = (p, q) if rows_first else (q, p)
            mid[HIDDEN * a : HIDDEN * a + HIDDEN, HIDDEN * b : HIDDEN * b + HIDDEN] = conv_mid_ref[p, q].astype(F32)
            out[40 * a : 40 * a + WEIGHTS, HIDDEN * b : HIDDEN * b + HIDDEN] = conv_out_ref[p, q].astype(F32)
    matrices[0][...] = in_t[...].T[0:HIDDEN].astype(BF16)
    matrices[1][...] = mid[...].astype(BF16)
    matrices[2][...] = out[...].astype(BF16)


def angle(coords, offset):
    return (coords + offset).astype(F32) * (2.0 * math.pi / DOMAIN)


def row_numbers(length, total):
    rows = lax.axis_index("gx") * ROWS - 8 + lax.broadcasted_iota(jnp.int32, (SPAN, length), 0)
    rows = jnp.where(rows < 0, rows + total, rows)
    return jnp.where(rows >= total, rows - total, rows)


def fill_tables(offsets_ref, table_ref, total):
    length = table_ref.shape[2]
    lanes = lax.broadcasted_iota(jnp.int32, (8, length), 1)
    layers = lax.broadcasted_iota(jnp.int32, (8, length), 0)
    rows = row_numbers(length, total)
    for axis in range(3):
        parts = [layers] if axis == 2 else [lanes, rows]
        coords = jnp.concatenate(parts, axis=0)
        turn = angle(coords, offsets_ref[axis])
        table_ref[2 * axis, 0 : turn.shape[0], :] = jnp.sin(turn)
        table_ref[2 * axis + 1, 0 : turn.shape[0], :] = jnp.cos(turn)


def fill_inputs(planes, u_ref, table_ref, row0, count, rows_first):
    length = u_ref.shape[3]

    def put(z, channel, q, values):
        put_rows(planes, z * count * INPUT_PITCH + 9 * q + channel, count, INPUT_PITCH, values)

    zero = jnp.zeros((DEPTH * count, length), F32)
    for spare in range(27, 32):
        put_rows(planes, spare, DEPTH * count, INPUT_PITCH, zero)
    row_axis, lane_axis = (1, 0) if rows_first else (0, 1)
    for part in range(2):
        rows = table_ref[2 * row_axis + part, 8 + row0 : 8 + row0 + count, :]
        row_of_lanes = table_ref[2 * lane_axis + part, 0:1, :]
        for z in range(DEPTH):
            layer = jnp.broadcast_to(table_ref[4 + part, z : z + 1, :], (count, length))
            for q in range(3):
                put(z, 3 + 2 * row_axis + part, q, rows)
                put(z, 7 + part, q, layer)
        for q in range(3):
            lanes = jnp.broadcast_to(roll_lanes(row_of_lanes, 1 - q), (count, length))
            for z in range(DEPTH):
                put(z, 3 + 2 * lane_axis + part, q, lanes)
    for c in range(3):
        for z in range(DEPTH):
            values = u_ref[c, 2 + z, row0 : row0 + count, :]
            for q in range(3):
                put(z, c, q, roll_lanes(values, 1 - q))


def gelu(x):
    half = 0.5 * x
    inner = x * (GELU_LINEAR + GELU_CUBIC * (x * x))
    return half + half * jnp.tanh(inner)


def spread(values, ref, row):
    length = values.shape[1] // DEPTH
    values = values.astype(BF16)
    ref[row, HIDDEN : 2 * HIDDEN, :] = values
    for z in range(DEPTH):
        lanes = slice(z * length, (z + 1) * length)
        ref[row, 0:HIDDEN, lanes] = roll_lanes(values[:, lanes], 1)
        ref[row, 2 * HIDDEN :, lanes] = roll_lanes(values[:, lanes], -1)


def tap_sums(matrix, ref, first, last, block, part, carry, emit):
    def body(step, state):
        base = first + step * block
        older = carry[0]
        newer = carry[1]
        for j in range(block):
            product = jnp.dot(matrix, ref[base + j], preferred_element_type=F32)
            emit(base + j, older + product[2 * part : 3 * part])
            older = newer + product[part : 2 * part]
            newer = product[0:part]
        carry[0] = older
        carry[1] = newer
        return state

    lax.fori_loop(0, (last - first) // block, body, 0)


def network(planes, stacked, first_ref, second_ref, carry_mid, carry_out, matrices, raw_ref, count, blocks, row0):
    length = stacked.shape[2] // DEPTH
    lanes = DEPTH * length
    matrix_in, matrix_mid, matrix_out = (m[...] for m in matrices)

    def stack(row):
        for z in range(DEPTH):
            start = (z * count + row) * INPUT_PITCH
            stacked[row, :, z * length : (z + 1) * length] = get_rows(planes, start, 32).astype(BF16)

    def first_row(row):
        operand = stacked[pl.ds(row, 3)].reshape(96, lanes)
        spread(gelu(jnp.dot(matrix_in, operand, preferred_element_type=F32)), first_ref, row)

    def emit_second(row, values):
        spread(gelu(values), second_ref, row)

    def emit_raw(row, values):
        for z in range(DEPTH):
            part = values[0:WEIGHTS, z * length : (z + 1) * length]
            for tile in range(lane_tiles(length)):
                raw_ref[tile, pl.ds(z * SPAN + row0 + row - 4, WEIGHTS, stride=WEIGHT_PITCH), :] = part[
                    :, 128 * tile : 128 * tile + 128
                ]

    if blocks is not None:
        for row in range(count):
            stack(row)

        def first_body(step, state):
            for j in range(blocks[0]):
                first_row(step * blocks[0] + j)
            return state

        lax.fori_loop(0, (count - 2) // blocks[0], first_body, 0)
        tap_sums(matrix_mid, first_ref, 0, count - 2, blocks[1], HIDDEN, carry_mid, emit_second)
        tap_sums(matrix_out, second_ref, 2, count - 2, blocks[2], 40, carry_out, emit_raw)
        return

    def rolling_sums(matrix, ref, first, part, emit):
        older = newer = None
        row = first
        while True:
            product = jnp.dot(matrix, ref[row], preferred_element_type=F32)
            if older is not None:
                emit(row, older + product[2 * part : 3 * part])
            older = None if newer is None else newer + product[part : 2 * part]
            newer = product[0:part]
            row += 1
            yield

    mid_rows = rolling_sums(matrix_mid, first_ref, 0, HIDDEN, emit_second)
    out_rows = rolling_sums(matrix_out, second_ref, 2, 40, emit_raw)
    stack(0)
    stack(1)
    for step in range(count - 2 + LAGS[1]):
        if step < count - 2:
            stack(step + 2)
            first_row(step)
        if LAGS[0] <= step < count - 2 + LAGS[0]:
            next(mid_rows)
        if LAGS[1] + 2 <= step:
            next(out_rows)


def at(ref, k, z, row, count):
    return get_rows(ref, k * WEIGHT_PITCH + z * SPAN + row, count)


def nearby(ref, c, z, row, count, direction, row_direction, steps):
    if direction == 2:
        return {t: ref[c, 2 + z + t, row : row + count, :] for t in steps}
    if direction == row_direction:
        return {t: ref[c, 2 + z, row + t : row + t + count, :] for t in steps}
    centre = ref[c, 2 + z, row : row + count, :]
    return {t: roll_lanes(centre, -t) for t in steps}


def speeds(ref, z, row, count, direction, row_direction):
    u = nearby(ref, direction, z, row, count, direction, row_direction, (-1, 0, 1))
    return 0.5 * (u[0] + u[1]), 0.5 * (u[0] + u[-1])


def advect(u_ref, w_ref, row, count, row_direction, from_raw, emit):
    for z in range(DEPTH):
        pace = [speeds(u_ref, z, row, count, d, row_direction) for d in range(3)]
        for c in range(3):
            change = None
            for d in range(3):
                taps = [at(w_ref, 12 * c + 4 * d + s, z, row, count) for s in range(4)]
                if from_raw:
                    mean = 0.25 * ((taps[0] + taps[1]) + (taps[2] + taps[3]))
                    for s in range(4):
                        taps[s] = (BASE_TAPS[s] + SPREAD * (taps[s] - mean)).astype(BF16).astype(F32)
                        put_rows(w_ref, (12 * c + 4 * d + s) * WEIGHT_PITCH + z * SPAN + row, count, 1, taps[s])
                u = nearby(u_ref, c, z, row, count, d, row_direction, (-2, -1, 0, 1, 2))
                up = (taps[0] * u[-1] + taps[1] * u[0]) + (taps[2] * u[1] + taps[3] * u[2])
                down = (taps[0] * u[-2] + taps[1] * u[-1]) + (taps[2] * u[0] + taps[3] * u[1])
                term = pace[d][0] * up - pace[d][1] * down
                change = term if change is None else change + term
            centre = u_ref[c, 2 + z, row : row + count, :]
            emit(c, z, row, count, centre - STEP_SIZE * change)


def y_kernel(
    total,
    offsets_ref,
    even_ref,
    odd_ref,
    velocity_ref,
    conv_in_ref,
    conv_mid_ref,
    conv_out_ref,
    stencil_ref,
    start_ref,
    middle_ref,
    table_ref,
    x_in_ref,
    x_mid_ref,
    x_out_ref,
    planes,
    stacked,
    first_ref,
    second_ref,
    carry_mid,
    carry_out,
    in_ref,
    mid_ref,
    out_ref,
    in_wide,
    mid_wide,
    out_wide,
):
    wide = (in_wide, mid_wide, out_wide)
    fill_tables(offsets_ref, table_ref, total)
    fill_weights(conv_in_ref, conv_mid_ref, conv_out_ref, wide, (in_ref, mid_ref, out_ref), True)
    fill_weights(conv_in_ref, conv_mid_ref, conv_out_ref, wide, (x_in_ref, x_mid_ref, x_out_ref), False)
    is_even = lax.rem(lax.axis_index("gx"), 2) == 0
    for c in range(3):
        for z in range(2 * DEPTH):
            pair = even_ref[c, z].astype(F32)
            other = odd_ref[c, z].astype(F32)
            start_ref[c, z, 0:8, :] = jnp.where(is_even, other, pair)
            start_ref[c, z, 16:24, :] = jnp.where(is_even, pair, other)
    for c in range(3):
        for z in range(2 * DEPTH):
            start_ref[c, z, 8:16, :] = velocity_ref[c, z].astype(F32)
    fill_inputs(planes, start_ref, table_ref, 1, 22, True)
    network(
        planes,
        stacked,
        first_ref,
        second_ref,
        carry_mid,
        carry_out,
        (in_ref, mid_ref, out_ref),
        stencil_ref,
        22,
        None if table_ref.shape[2] <= 128 else (5, 5, 6),
        4,
    )

    def emit(c, z, row, count, values):
        middle_ref[c, 2 + z, row : row + count, :] = values

    for row in (4, 12):
        advect(start_ref, stencil_ref, row, 8, 1, True, emit)
    for c in range(3):
        for z in (0, 1, 6, 7):
            middle_ref[c, z] = start_ref[c, z]


def adjoint_terms(u_ref, w_ref, g_ref, z, row, count, direction, put, grads):
    up_speed, down_speed = speeds(u_ref, z, row, count, direction, 1)
    into_up = None
    parts = []
    for c in range(3):
        scaled = -STEP_SIZE * g_ref[c, z, row : row + count, :]
        u = nearby(u_ref, c, z, row, count, direction, 1, (-2, -1, 0, 1, 2))
        h_up = scaled * up_speed
        h_down = scaled * down_speed
        if grads is not None:
            for s in range(4):
                grads(12 * c + 4 * direction + s, z, h_up * u[s - 1] - h_down * u[s - 2])
        if put is None:
            continue
        w = [at(w_ref, 12 * c + 4 * direction + s, z, row, count) for s in range(4)]
        up = (w[0] * u[-1] + w[1] * u[0]) + (w[2] * u[1] + w[3] * u[2])
        down = (w[0] * u[-2] + w[1] * u[-1]) + (w[2] * u[0] + w[3] * u[1])
        if into_up is None:
            into_up = scaled * up
            into_down = scaled * down
        else:
            into_up = into_up + scaled * up
            into_down = into_down + scaled * down
        parts.append(
            {
                -2: -h_down * w[0],
                -1: h_up * w[0] - h_down * w[1],
                0: h_up * w[1] - h_down * w[2],
                1: h_up * w[2] - h_down * w[3],
                2: h_up * w[3],
            }
        )
    if put is not None:
        own = parts[direction]
        own[0] = own[0] + 0.5 * (into_up - into_down)
        own[1] = own[1] + 0.5 * into_up
        own[-1] = own[-1] - 0.5 * into_down
        for c in range(3):
            put(c, parts[c])


def x_kernel(
    received_ref,
    stencil_ref,
    start_ref,
    middle_ref,
    table_ref,
    in_ref,
    mid_ref,
    out_ref,
    final_ref,
    grads_ref,
    planes,
    stacked,
    first_ref,
    second_ref,
    carry_mid,
    carry_out,
    own_ref,
    turned_ref,
    back_ref,
    raw_ref,
    next_ref,
    block_ref,
):
    length = start_ref.shape[3]

    def group(g):
        half = received_ref[:, 16 * (g // 2) : 16 * (g // 2) + 16, :].astype(F32)
        half = half[:, 8 * (g % 2) : 8 * (g % 2) + 8, :]
        return half.reshape(length, 128).T

    ghost_layers = [(c, z) for c in range(3) for z in (0, 1, 6, 7)]
    targets = [(own_ref, c, 2 + z, 3) for c in range(3) for z in range(DEPTH)]
    targets += [(own_ref, c, z, 6) for c, z in ghost_layers]
    targets += [(turned_ref, c, z, 6) for c in range(3) for z in range(DEPTH)]
    for g, places in enumerate(message_places()):
        block_ref[...] = group(g)
        for plane, first, lanes, skipped in places:
            ref, c, z, row = targets[plane]
            ref[c, z, row + skipped : row + skipped + lanes, :] = block_ref[first : first + lanes, :]

    for c in range(3):
        for z in range(DEPTH):
            back_ref[c, z, 8:16, :] = turned_ref[c, z, 8:16, :]

    def keep(k, z, values):
        put_rows(raw_ref, k * WEIGHT_PITCH + z * SPAN, ROWS, 1, values)

    for direction in range(3):
        blocks = ((8, 8, keep), (6, 2, None), (16, 2, None)) if direction == 1 else ((8, 8, keep),)
        for row, count, grads in blocks:
            for z in range(DEPTH):

                def put(c, parts):
                    if direction == 0:
                        total_part = parts[0]
                        for t in (-2, -1, 1, 2):
                            total_part = total_part + roll_lanes(parts[t], t)
                        back_ref[c, z, 8:16, :] += total_part
                    elif direction == 2:
                        for t in (-2, -1, 0, 1, 2):
                            if 0 <= z + t < DEPTH:
                                back_ref[c, z + t, 8:16, :] += parts[t]
                    else:
                        for t in (-2, -1, 0, 1, 2):
                            back_ref[c, z, row + t : row + t + count, :] += parts[t]

                adjoint_terms(middle_ref, stencil_ref, turned_ref, z, row, count, direction, put, grads)

    def finish(k, z, values):
        later = get_rows(raw_ref, k * WEIGHT_PITCH + z * SPAN, ROWS)
        grads_ref[k, z] = (later + values).astype(BF16)

    for direction in range(3):
        for z in range(DEPTH):
            adjoint_terms(start_ref, stencil_ref, back_ref, z, 8, 8, direction, None, finish)

    fill_inputs(planes, own_ref, table_ref, 3, 18, False)
    network(
        planes,
        stacked,
        first_ref,
        second_ref,
        carry_mid,
        carry_out,
        (in_ref, mid_ref, out_ref),
        raw_ref,
        18,
        None if table_ref.shape[2] <= 128 else (4, 4, 7),
        6,
    )

    def emit_middle(c, z, row, count, values):
        next_ref[c, 2 + z, row : row + count, :] = values

    for row, count in ((6, 8), (14, 4)):
        advect(own_ref, raw_ref, row, count, 0, True, emit_middle)
    for c, z in ghost_layers:
        next_ref[c, z, 8:16, :] = own_ref[c, z, 8:16, :]

    def emit_final(c, z, row, count, values):
        final_ref[c, z] = values

    advect(next_ref, raw_ref, 8, 8, 0, False, emit_final)


def network_scratch(count, length):
    lanes = DEPTH * length
    return [
        pltpu.VMEM((lane_tiles(length), DEPTH * count * INPUT_PITCH, 128), F32),
        pltpu.VMEM((count, 32, lanes), BF16),
        pltpu.VMEM((count - 2, 3 * HIDDEN, lanes), BF16),
        pltpu.VMEM((count - 2, 3 * HIDDEN, lanes), BF16),
        pltpu.VMEM((2, HIDDEN, lanes), F32),
        pltpu.VMEM((2, 40, lanes), F32),
    ]


def on_device(velocity, offsets, conv_in, conv_mid, conv_out, cotangent):
    devices = lax.axis_size("gx")
    length = velocity.shape[3]
    assert velocity.shape[2] == ROWS and velocity.shape[1] == 2 * DEPTH and length == ROWS * devices
    pairs = [(i, i ^ 1) for i in range(devices)]
    others = [(i, (i + 1) % devices if i % 2 else (i - 1) % devices) for i in range(devices)]
    odd = lax.ppermute(velocity, "gx", others)
    even = lax.ppermute(velocity, "gx", pairs)
    vmem = pl.BlockSpec(memory_space=pltpu.VMEM)
    smem = pl.BlockSpec(memory_space=pltpu.SMEM)
    in_taps = jnp.transpose(conv_in, (1, 2, 3, 0))
    mid_taps = jnp.transpose(conv_mid, (2, 3, 0, 1))
    out_taps = jnp.transpose(conv_out, (2, 3, 0, 1))
    slab = (3, 2 * DEPTH, SPAN, length)
    weights = (lane_tiles(length), WEIGHTS * WEIGHT_PITCH, 128)
    matrices = (((HIDDEN, 96), BF16), ((3 * HIDDEN, 3 * HIDDEN), BF16), ((120, 3 * HIDDEN), BF16))
    local = [pltpu.with_memory_space_constraint(a, pltpu.HBM) for a in (velocity, in_taps, mid_taps, out_taps)]
    send = pl.pallas_call(
        functools.partial(pack_kernel, devices),
        out_shape=jax.ShapeDtypeStruct((devices, PACKED, 128), BF16),
        in_specs=[vmem] * 2,
        out_specs=vmem,
        compiler_params=pltpu.CompilerParams(vmem_limit_bytes=24 << 20),
        name="pack",
    )(local[0], pltpu.with_memory_space_constraint(cotangent, pltpu.HBM))
    received = lax.all_to_all(send, "gx", 0, 0)
    limit = pltpu.CompilerParams(vmem_limit_bytes=(24 if length <= 128 else 61) << 20)
    stencil, start, middle, *tables = pl.pallas_call(
        functools.partial(y_kernel, length),
        out_shape=tuple(
            jax.ShapeDtypeStruct(*shape)
            for shape in ((weights, F32), (slab, F32), (slab, F32), ((6, 8 + SPAN, length), F32)) + matrices
        ),
        in_specs=[smem] + [vmem] * 6,
        out_specs=(vmem,) * 7,
        scratch_shapes=network_scratch(22, length)
        + [pltpu.VMEM(*shape) for shape in matrices]
        + [
            pltpu.VMEM((96, 128), F32),
            pltpu.VMEM((3 * HIDDEN, 3 * HIDDEN), F32),
            pltpu.VMEM((120, 3 * HIDDEN), F32),
        ],
        compiler_params=limit,
        cost_estimate=pl.CostEstimate(flops=4 * 10**9, transcendentals=10**6, bytes_accessed=10**7),
        name="y_slab",
    )(pltpu.with_memory_space_constraint(offsets, pltpu.HBM), even, odd, *local)
    final_state, weight_grads = pl.pallas_call(
        x_kernel,
        out_shape=(
            jax.ShapeDtypeStruct((3, DEPTH, ROWS, length), F32),
            jax.ShapeDtypeStruct((WEIGHTS, DEPTH, ROWS, length), BF16),
        ),
        in_specs=[vmem] * 8,
        out_specs=(vmem, vmem),
        scratch_shapes=network_scratch(18, length)
        + [
            pltpu.VMEM(slab, F32),
            pltpu.VMEM((3, DEPTH, SPAN, length), F32),
            pltpu.VMEM((3, DEPTH, SPAN, length), F32),
            pltpu.VMEM(weights, F32),
            pltpu.VMEM(slab, F32),
            pltpu.VMEM((128, length), F32),
        ],
        compiler_params=limit,
        cost_estimate=pl.CostEstimate(flops=3 * 10**9, transcendentals=10**6, bytes_accessed=10**7),
        name="x_slab",
    )(received, stencil, start, middle, *tables)
    return (final_state, weight_grads)


def solution(mesh):
    return jax.shard_map(
        on_device,
        mesh=mesh,
        in_specs=(
            P(None, "groups", "gx", None),
            P("groups"),
            P(),
            P(),
            P(),
            P(None, "groups", "gx", None),
        ),
        out_specs=(P(None, "groups", "gx", None), P(None, "groups", "gx", None)),
        check_vma=False,
    )
```

```python
import functools
import math

import jax
import jax.numpy as jnp
from jax import lax
from jax.experimental import pallas as pl
from jax.experimental.pallas import tpu as pltpu
from jax.sharding import PartitionSpec as P

DOMAIN = 1024
SPREAD = 0.25
STEP_SIZE = 0.3
BASE_TAPS = (-0.0625, 0.5625, 0.5625, -0.0625)

GELU_LINEAR = math.sqrt(2.0 / math.pi)
GELU_CUBIC = 0.044715 * GELU_LINEAR

DEPTH = 4
ROWS = 8
SPAN = 24
HIDDEN = 64
WEIGHTS = 36
INPUT_PITCH = 33
LAGS = (20, 40)
WEIGHT_PITCH = DEPTH * SPAN + 1
PACKED = 32
F32 = jnp.float32
BF16 = jnp.bfloat16


def lane_tiles(length):
    return length // 128


def put_rows(ref, start, count, stride, values):
    for tile in range(ref.shape[0]):
        part = values[:, 128 * tile : 128 * tile + 128]
        if stride == 1:
            ref[tile, start : start + count, :] = part
        else:
            ref[tile, pl.ds(start, count, stride=stride), :] = part


def get_rows(ref, start, count):
    parts = [ref[tile, start : start + count, :] for tile in range(ref.shape[0])]
    return parts[0] if len(parts) == 1 else jnp.concatenate(parts, axis=1)


def roll_lanes(values, shift):
    width = values.shape[-1]
    shift = shift % width
    if shift == 0:
        return values
    return pltpu.roll(values, shift, values.ndim - 1)


def message_places():
    places = [[(p, 18 * p, 18, 0) for p in range(7)]]
    places.append([(7 + p, 18 * p, 18, 0) for p in range(5)] + [(12 + p, 90 + 12 * p, 12, 0) for p in range(3)])
    places.append([(15 + p, 12 * p, 12, 0) for p in range(10)] + [(35, 120, 8, 0)])
    places.append([(25 + p, 12 * p, 12, 0) for p in range(10)] + [(35, 120, 4, 8)])
    return places


def pack_kernel(devices, velocity_ref, cotangent_ref, send_ref):
    length = velocity_ref.shape[3]
    planes = [velocity_ref[c, 2 + z].astype(F32) for c in range(3) for z in range(DEPTH)]
    planes += [velocity_ref[c, z].astype(F32) for c in range(3) for z in (0, 1, 6, 7)]
    planes += [cotangent_ref[c, z] for c in range(3) for z in range(DEPTH)]
    groups = []
    for places in message_places():
        members = []
        for plane, first, lanes, skipped in places:
            halo = 5 if plane < 12 else 2
            members.append((roll_lanes(planes[plane], first - skipped + halo), first))
        groups.append(members)
    lane = lax.broadcasted_iota(jnp.int32, (ROWS, length), 1)

    def one(dest):
        place = lane - ROWS * dest
        place = jnp.where(place < 0, place + length, place)
        done = []
        for members in groups:
            mixed = members[0][0]
            for values, first in members[1:]:
                mixed = jnp.where(place < first, mixed, values)
            if isinstance(dest, int):
                moved = roll_lanes(mixed, -ROWS * dest)
            else:
                moved = pltpu.roll(mixed, length - ROWS * dest, 1)
            done.append(moved[:, 0:128])
        for pair in range(2):
            both = jnp.concatenate([done[2 * pair], done[2 * pair + 1]], axis=0)
            send_ref[dest, 16 * pair : 16 * pair + 16, :] = both.astype(BF16)

    if devices <= 16:
        for dest in range(devices):
            one(dest)
    else:

        def body(dest, carry):
            one(dest)
            return carry

        lax.fori_loop(0, devices, body, 0)


def fill_weights(conv_in_ref, conv_mid_ref, conv_out_ref, scratch, matrices, rows_first):
    in_t, mid, out = scratch
    in_t[...] = jnp.zeros_like(in_t)
    for i in range(9):
        for p in range(3):
            taps = conv_in_ref[i, p].astype(F32)
            if rows_first:
                in_t[pl.ds(32 * p + i, 3, stride=9), 0:HIDDEN] = taps
            else:
                in_t[pl.ds(9 * p + i, 3, stride=32), 0:HIDDEN] = taps
    for p in range(3):
        for q in range(3):
            a, b = (p, q) if rows_first else (q, p)
            mid[HIDDEN * a : HIDDEN * a + HIDDEN, HIDDEN * b : HIDDEN * b + HIDDEN] = conv_mid_ref[p, q].astype(F32)
            out[40 * a : 40 * a + WEIGHTS, HIDDEN * b : HIDDEN * b + HIDDEN] = conv_out_ref[p, q].astype(F32)
    matrices[0][...] = in_t[...].T[0:HIDDEN].astype(BF16)
    matrices[1][...] = mid[...].astype(BF16)
    matrices[2][...] = out[...].astype(BF16)


def angle(coords, offset):
    return (coords + offset).astype(F32) * (2.0 * math.pi / DOMAIN)


def row_numbers(length, total):
    rows = lax.axis_index("gx") * ROWS - 8 + lax.broadcasted_iota(jnp.int32, (SPAN, length), 0)
    rows = jnp.where(rows < 0, rows + total, rows)
    return jnp.where(rows >= total, rows - total, rows)


def fill_tables(offsets_ref, table_ref, total):
    length = table_ref.shape[2]
    lanes = lax.broadcasted_iota(jnp.int32, (8, length), 1)
    layers = lax.broadcasted_iota(jnp.int32, (8, length), 0)
    rows = row_numbers(length, total)
    for axis in range(3):
        parts = [layers] if axis == 2 else [lanes, rows]
        coords = jnp.concatenate(parts, axis=0)
        turn = angle(coords, offsets_ref[axis])
        table_ref[2 * axis, 0 : turn.shape[0], :] = jnp.sin(turn)
        table_ref[2 * axis + 1, 0 : turn.shape[0], :] = jnp.cos(turn)


def fill_inputs(planes, u_ref, table_ref, row0, count, rows_first):
    length = u_ref.shape[3]

    def put(z, channel, q, values):
        put_rows(planes, z * count * INPUT_PITCH + 9 * q + channel, count, INPUT_PITCH, values)

    zero = jnp.zeros((DEPTH * count, length), F32)
    for spare in range(27, 32):
        put_rows(planes, spare, DEPTH * count, INPUT_PITCH, zero)
    row_axis, lane_axis = (1, 0) if rows_first else (0, 1)
    for part in range(2):
        rows = table_ref[2 * row_axis + part, 8 + row0 : 8 + row0 + count, :]
        row_of_lanes = table_ref[2 * lane_axis + part, 0:1, :]
        for z in range(DEPTH):
            layer = jnp.broadcast_to(table_ref[4 + part, z : z + 1, :], (count, length))
            for q in range(3):
                put(z, 3 + 2 * row_axis + part, q, rows)
                put(z, 7 + part, q, layer)
        for q in range(3):
            lanes = jnp.broadcast_to(roll_lanes(row_of_lanes, 1 - q), (count, length))
            for z in range(DEPTH):
                put(z, 3 + 2 * lane_axis + part, q, lanes)
    for c in range(3):
        for z in range(DEPTH):
            values = u_ref[c, 2 + z, row0 : row0 + count, :]
            for q in range(3):
                put(z, c, q, roll_lanes(values, 1 - q))


def gelu(x):
    half = 0.5 * x
    inner = x * (GELU_LINEAR + GELU_CUBIC * (x * x))
    return half + half * jnp.tanh(inner)


def spread(values, ref, row):
    length = values.shape[1] // DEPTH
    values = values.astype(BF16)
    ref[row, HIDDEN : 2 * HIDDEN, :] = values
    for z in range(DEPTH):
        lanes = slice(z * length, (z + 1) * length)
        ref[row, 0:HIDDEN, lanes] = roll_lanes(values[:, lanes], 1)
        ref[row, 2 * HIDDEN :, lanes] = roll_lanes(values[:, lanes], -1)


def tap_sums(matrix, ref, first, last, block, part, carry, emit):
    def body(step, state):
        base = first + step * block
        older = carry[0]
        newer = carry[1]
        for j in range(block):
            product = jnp.dot(matrix, ref[base + j], preferred_element_type=F32)
            emit(base + j, older + product[2 * part : 3 * part])
            older = newer + product[part : 2 * part]
            newer = product[0:part]
        carry[0] = older
        carry[1] = newer
        return state

    lax.fori_loop(0, (last - first) // block, body, 0)


def network(planes, stacked, first_ref, second_ref, carry_mid, carry_out, matrices, raw_ref, count, blocks, row0):
    length = stacked.shape[2] // DEPTH
    lanes = DEPTH * length
    matrix_in, matrix_mid, matrix_out = (m[...] for m in matrices)

    def stack(row):
        for z in range(DEPTH):
            start = (z * count + row) * INPUT_PITCH
            stacked[row, :, z * length : (z + 1) * length] = get_rows(planes, start, 32).astype(BF16)

    def first_row(row):
        operand = stacked[pl.ds(row, 3)].reshape(96, lanes)
        spread(gelu(jnp.dot(matrix_in, operand, preferred_element_type=F32)), first_ref, row)

    def emit_second(row, values):
        spread(gelu(values), second_ref, row)

    def emit_raw(row, values):
        for z in range(DEPTH):
            part = values[0:WEIGHTS, z * length : (z + 1) * length]
            for tile in range(lane_tiles(length)):
                raw_ref[tile, pl.ds(z * SPAN + row0 + row - 4, WEIGHTS, stride=WEIGHT_PITCH), :] = part[
                    :, 128 * tile : 128 * tile + 128
                ]

    if blocks is not None:
        for row in range(count):
            stack(row)

        def first_body(step, state):
            for j in range(blocks[0]):
                first_row(step * blocks[0] + j)
            return state

        lax.fori_loop(0, (count - 2) // blocks[0], first_body, 0)
        tap_sums(matrix_mid, first_ref, 0, count - 2, blocks[1], HIDDEN, carry_mid, emit_second)
        tap_sums(matrix_out, second_ref, 2, count - 2, blocks[2], 40, carry_out, emit_raw)
        return

    def rolling_sums(matrix, ref, first, part, emit):
        older = newer = None
        row = first
        while True:
            product = jnp.dot(matrix, ref[row], preferred_element_type=F32)
            if older is not None:
                emit(row, older + product[2 * part : 3 * part])
            older = None if newer is None else newer + product[part : 2 * part]
            newer = product[0:part]
            row += 1
            yield

    mid_rows = rolling_sums(matrix_mid, first_ref, 0, HIDDEN, emit_second)
    out_rows = rolling_sums(matrix_out, second_ref, 2, 40, emit_raw)
    stack(0)
    stack(1)
    for step in range(count - 2 + LAGS[1]):
        if step < count - 2:
            stack(step + 2)
            first_row(step)
        if LAGS[0] <= step < count - 2 + LAGS[0]:
            next(mid_rows)
        if LAGS[1] + 2 <= step:
            next(out_rows)


def at(ref, k, z, row, count):
    return get_rows(ref, k * WEIGHT_PITCH + z * SPAN + row, count)


def nearby(ref, c, z, row, count, direction, row_direction, steps):
    if direction == 2:
        return {t: ref[c, 2 + z + t, row : row + count, :] for t in steps}
    if direction == row_direction:
        return {t: ref[c, 2 + z, row + t : row + t + count, :] for t in steps}
    centre = ref[c, 2 + z, row : row + count, :]
    return {t: roll_lanes(centre, -t) for t in steps}


def speeds(ref, z, row, count, direction, row_direction):
    u = nearby(ref, direction, z, row, count, direction, row_direction, (-1, 0, 1))
    return 0.5 * (u[0] + u[1]), 0.5 * (u[0] + u[-1])


def advect(u_ref, w_ref, row, count, row_direction, from_raw, emit):
    for z in range(DEPTH):
        pace = [speeds(u_ref, z, row, count, d, row_direction) for d in range(3)]
        for c in range(3):
            change = None
            for d in range(3):
                taps = [at(w_ref, 12 * c + 4 * d + s, z, row, count) for s in range(4)]
                if from_raw:
                    mean = 0.25 * ((taps[0] + taps[1]) + (taps[2] + taps[3]))
                    for s in range(4):
                        taps[s] = (BASE_TAPS[s] + SPREAD * (taps[s] - mean)).astype(BF16).astype(F32)
                        put_rows(w_ref, (12 * c + 4 * d + s) * WEIGHT_PITCH + z * SPAN + row, count, 1, taps[s])
                u = nearby(u_ref, c, z, row, count, d, row_direction, (-2, -1, 0, 1, 2))
                up = (taps[0] * u[-1] + taps[1] * u[0]) + (taps[2] * u[1] + taps[3] * u[2])
                down = (taps[0] * u[-2] + taps[1] * u[-1]) + (taps[2] * u[0] + taps[3] * u[1])
                term = pace[d][0] * up - pace[d][1] * down
                change = term if change is None else change + term
            centre = u_ref[c, 2 + z, row : row + count, :]
            emit(c, z, row, count, centre - STEP_SIZE * change)


def y_kernel(
    total,
    offsets_ref,
    even_ref,
    odd_ref,
    velocity_ref,
    conv_in_ref,
    conv_mid_ref,
    conv_out_ref,
    stencil_ref,
    start_ref,
    middle_ref,
    table_ref,
    x_in_ref,
    x_mid_ref,
    x_out_ref,
    planes,
    stacked,
    first_ref,
    second_ref,
    carry_mid,
    carry_out,
    in_ref,
    mid_ref,
    out_ref,
    in_wide,
    mid_wide,
    out_wide,
):
    wide = (in_wide, mid_wide, out_wide)
    fill_tables(offsets_ref, table_ref, total)
    fill_weights(conv_in_ref, conv_mid_ref, conv_out_ref, wide, (in_ref, mid_ref, out_ref), True)
    fill_weights(conv_in_ref, conv_mid_ref, conv_out_ref, wide, (x_in_ref, x_mid_ref, x_out_ref), False)
    is_even = lax.rem(lax.axis_index("gx"), 2) == 0
    for c in range(3):
        for z in range(2 * DEPTH):
            pair = even_ref[c, z].astype(F32)
            other = odd_ref[c, z].astype(F32)
            start_ref[c, z, 0:8, :] = jnp.where(is_even, other, pair)
            start_ref[c, z, 16:24, :] = jnp.where(is_even, pair, other)
    for c in range(3):
        for z in range(2 * DEPTH):
            start_ref[c, z, 8:16, :] = velocity_ref[c, z].astype(F32)
    fill_inputs(planes, start_ref, table_ref, 1, 22, True)
    network(
        planes,
        stacked,
        first_ref,
        second_ref,
        carry_mid,
        carry_out,
        (in_ref, mid_ref, out_ref),
        stencil_ref,
        22,
        None if table_ref.shape[2] <= 128 else (5, 5, 6),
        4,
    )

    def emit(c, z, row, count, values):
        middle_ref[c, 2 + z, row : row + count, :] = values

    for row in (4, 12):
        advect(start_ref, stencil_ref, row, 8, 1, True, emit)
    for c in range(3):
        for z in (0, 1, 6, 7):
            middle_ref[c, z] = start_ref[c, z]


def adjoint_terms(u_ref, w_ref, g_ref, z, row, count, direction, put, grads):
    up_speed, down_speed = speeds(u_ref, z, row, count, direction, 1)
    into_up = None
    parts = []
    for c in range(3):
        scaled = -STEP_SIZE * g_ref[c, z, row : row + count, :]
        u = nearby(u_ref, c, z, row, count, direction, 1, (-2, -1, 0, 1, 2))
        h_up = scaled * up_speed
        h_down = scaled * down_speed
        if grads is not None:
            for s in range(4):
                grads(12 * c + 4 * direction + s, z, h_up * u[s - 1] - h_down * u[s - 2])
        if put is None:
            continue
        w = [at(w_ref, 12 * c + 4 * direction + s, z, row, count) for s in range(4)]
        up = (w[0] * u[-1] + w[1] * u[0]) + (w[2] * u[1] + w[3] * u[2])
        down = (w[0] * u[-2] + w[1] * u[-1]) + (w[2] * u[0] + w[3] * u[1])
        if into_up is None:
            into_up = scaled * up
            into_down = scaled * down
        else:
            into_up = into_up + scaled * up
            into_down = into_down + scaled * down
        parts.append(
            {
                -2: -h_down * w[0],
                -1: h_up * w[0] - h_down * w[1],
                0: h_up * w[1] - h_down * w[2],
                1: h_up * w[2] - h_down * w[3],
                2: h_up * w[3],
            }
        )
    if put is not None:
        own = parts[direction]
        own[0] = own[0] + 0.5 * (into_up - into_down)
        own[1] = own[1] + 0.5 * into_up
        own[-1] = own[-1] - 0.5 * into_down
        for c in range(3):
            put(c, parts[c])


def x_kernel(
    received_ref,
    stencil_ref,
    start_ref,
    middle_ref,
    table_ref,
    in_ref,
    mid_ref,
    out_ref,
    final_ref,
    grads_ref,
    planes,
    stacked,
    first_ref,
    second_ref,
    carry_mid,
    carry_out,
    own_ref,
    turned_ref,
    back_ref,
    raw_ref,
    next_ref,
    block_ref,
):
    length = start_ref.shape[3]

    def group(g):
        half = received_ref[:, 16 * (g // 2) : 16 * (g // 2) + 16, :].astype(F32)
        half = half[:, 8 * (g % 2) : 8 * (g % 2) + 8, :]
        return half.reshape(length, 128).T

    ghost_layers = [(c, z) for c in range(3) for z in (0, 1, 6, 7)]
    targets = [(own_ref, c, 2 + z, 3) for c in range(3) for z in range(DEPTH)]
    targets += [(own_ref, c, z, 6) for c, z in ghost_layers]
    targets += [(turned_ref, c, z, 6) for c in range(3) for z in range(DEPTH)]
    for g, places in enumerate(message_places()):
        block_ref[...] = group(g)
        for plane, first, lanes, skipped in places:
            ref, c, z, row = targets[plane]
            ref[c, z, row + skipped : row + skipped + lanes, :] = block_ref[first : first + lanes, :]

    for c in range(3):
        for z in range(DEPTH):
            back_ref[c, z, 8:16, :] = turned_ref[c, z, 8:16, :]

    def keep(k, z, values):
        put_rows(raw_ref, k * WEIGHT_PITCH + z * SPAN, ROWS, 1, values)

    for direction in range(3):
        blocks = ((8, 8, keep), (6, 2, None), (16, 2, None)) if direction == 1 else ((8, 8, keep),)
        for row, count, grads in blocks:
            for z in range(DEPTH):

                def put(c, parts):
                    if direction == 0:
                        total_part = parts[0]
                        for t in (-2, -1, 1, 2):
                            total_part = total_part + roll_lanes(parts[t], t)
                        back_ref[c, z, 8:16, :] += total_part
                    elif direction == 2:
                        for t in (-2, -1, 0, 1, 2):
                            if 0 <= z + t < DEPTH:
                                back_ref[c, z + t, 8:16, :] += parts[t]
                    else:
                        for t in (-2, -1, 0, 1, 2):
                            back_ref[c, z, row + t : row + t + count, :] += parts[t]

                adjoint_terms(middle_ref, stencil_ref, turned_ref, z, row, count, direction, put, grads)

    def finish(k, z, values):
        later = get_rows(raw_ref, k * WEIGHT_PITCH + z * SPAN, ROWS)
        grads_ref[k, z] = (later + values).astype(BF16)

    for direction in range(3):
        for z in range(DEPTH):
            adjoint_terms(start_ref, stencil_ref, back_ref, z, 8, 8, direction, None, finish)

    fill_inputs(planes, own_ref, table_ref, 3, 18, False)
    network(
        planes,
        stacked,
        first_ref,
        second_ref,
        carry_mid,
        carry_out,
        (in_ref, mid_ref, out_ref),
        raw_ref,
        18,
        None if table_ref.shape[2] <= 128 else (4, 4, 7),
        6,
    )

    def emit_middle(c, z, row, count, values):
        next_ref[c, 2 + z, row : row + count, :] = values

    for row, count in ((6, 8), (14, 4)):
        advect(own_ref, raw_ref, row, count, 0, True, emit_middle)
    for c, z in ghost_layers:
        next_ref[c, z, 8:16, :] = own_ref[c, z, 8:16, :]

    def emit_final(c, z, row, count, values):
        final_ref[c, z] = values

    advect(next_ref, raw_ref, 8, 8, 0, False, emit_final)


def network_scratch(count, length):
    lanes = DEPTH * length
    return [
        pltpu.VMEM((lane_tiles(length), DEPTH * count * INPUT_PITCH, 128), F32),
        pltpu.VMEM((count, 32, lanes), BF16),
        pltpu.VMEM((count - 2, 3 * HIDDEN, lanes), BF16),
        pltpu.VMEM((count - 2, 3 * HIDDEN, lanes), BF16),
        pltpu.VMEM((2, HIDDEN, lanes), F32),
        pltpu.VMEM((2, 40, lanes), F32),
    ]


def on_device(velocity, offsets, conv_in, conv_mid, conv_out, cotangent):
    devices = lax.axis_size("gx")
    length = velocity.shape[3]
    assert velocity.shape[2] == ROWS and velocity.shape[1] == 2 * DEPTH and length == ROWS * devices
    pairs = [(i, i ^ 1) for i in range(devices)]
    others = [(i, (i + 1) % devices if i % 2 else (i - 1) % devices) for i in range(devices)]
    vmem = pl.BlockSpec(memory_space=pltpu.VMEM)
    smem = pl.BlockSpec(memory_space=pltpu.SMEM)
    in_taps = jnp.transpose(conv_in, (1, 2, 3, 0))
    mid_taps = jnp.transpose(conv_mid, (2, 3, 0, 1))
    out_taps = jnp.transpose(conv_out, (2, 3, 0, 1))
    slab = (3, 2 * DEPTH, SPAN, length)
    weights = (lane_tiles(length), WEIGHTS * WEIGHT_PITCH, 128)
    matrices = (((HIDDEN, 96), BF16), ((3 * HIDDEN, 3 * HIDDEN), BF16), ((120, 3 * HIDDEN), BF16))
    local = [pltpu.with_memory_space_constraint(a, pltpu.HBM) for a in (velocity, in_taps, mid_taps, out_taps)]
    send = pl.pallas_call(
        functools.partial(pack_kernel, devices),
        out_shape=jax.ShapeDtypeStruct((devices, PACKED, 128), BF16),
        in_specs=[vmem] * 2,
        out_specs=vmem,
        compiler_params=pltpu.CompilerParams(vmem_limit_bytes=24 << 20),
        name="pack",
    )(local[0], pltpu.with_memory_space_constraint(cotangent, pltpu.HBM))
    moving, send = lax.optimization_barrier((velocity, send))
    received = lax.all_to_all(send, "gx", 0, 0)
    odd = lax.ppermute(moving, "gx", others)
    even = lax.ppermute(moving, "gx", pairs)
    limit = pltpu.CompilerParams(vmem_limit_bytes=(24 if length <= 128 else 61) << 20)
    stencil, start, middle, *tables = pl.pallas_call(
        functools.partial(y_kernel, length),
        out_shape=tuple(
            jax.ShapeDtypeStruct(*shape)
            for shape in ((weights, F32), (slab, F32), (slab, F32), ((6, 8 + SPAN, length), F32)) + matrices
        ),
        in_specs=[smem] + [vmem] * 6,
        out_specs=(vmem,) * 7,
        scratch_shapes=network_scratch(22, length)
        + [pltpu.VMEM(*shape) for shape in matrices]
        + [
            pltpu.VMEM((96, 128), F32),
            pltpu.VMEM((3 * HIDDEN, 3 * HIDDEN), F32),
            pltpu.VMEM((120, 3 * HIDDEN), F32),
        ],
        compiler_params=limit,
        cost_estimate=pl.CostEstimate(flops=4 * 10**9, transcendentals=10**6, bytes_accessed=10**7),
        name="y_slab",
    )(pltpu.with_memory_space_constraint(offsets, pltpu.HBM), even, odd, *local)
    final_state, weight_grads = pl.pallas_call(
        x_kernel,
        out_shape=(
            jax.ShapeDtypeStruct((3, DEPTH, ROWS, length), F32),
            jax.ShapeDtypeStruct((WEIGHTS, DEPTH, ROWS, length), BF16),
        ),
        in_specs=[vmem] * 8,
        out_specs=(vmem, vmem),
        scratch_shapes=network_scratch(18, length)
        + [
            pltpu.VMEM(slab, F32),
            pltpu.VMEM((3, DEPTH, SPAN, length), F32),
            pltpu.VMEM((3, DEPTH, SPAN, length), F32),
            pltpu.VMEM(weights, F32),
            pltpu.VMEM(slab, F32),
            pltpu.VMEM((128, length), F32),
        ],
        compiler_params=limit,
        cost_estimate=pl.CostEstimate(flops=3 * 10**9, transcendentals=10**6, bytes_accessed=10**7),
        name="x_slab",
    )(received, stencil, start, middle, *tables)
    return (final_state, weight_grads)


def solution(mesh):
    return jax.shard_map(
        on_device,
        mesh=mesh,
        in_specs=(
            P(None, "groups", "gx", None),
            P("groups"),
            P(),
            P(),
            P(),
            P(None, "groups", "gx", None),
        ),
        out_specs=(P(None, "groups", "gx", None), P(None, "groups", "gx", None)),
        check_vma=False,
    )
```

```python
import functools
import math

import jax
import jax.numpy as jnp
from jax import lax
from jax.experimental import pallas as pl
from jax.experimental.pallas import tpu as pltpu
from jax.sharding import PartitionSpec as P

DOMAIN = 1024
SPREAD = 0.25
STEP_SIZE = 0.3
BASE_TAPS = (-0.0625, 0.5625, 0.5625, -0.0625)

GELU_LINEAR = 2.0 * math.sqrt(2.0 / math.pi)
GELU_CUBIC = 4.0 * 0.044715 * GELU_LINEAR

DEPTH = 4
ROWS = 8
SPAN = 24
HIDDEN = 64
WEIGHTS = 36
INPUT_PITCH = 33
LAGS = (20, 40)
WEIGHT_PITCH = DEPTH * SPAN + 1
PACKED = 32
F32 = jnp.float32
BF16 = jnp.bfloat16


def lane_tiles(length):
    return length // 128


def put_rows(ref, start, count, stride, values):
    for tile in range(ref.shape[0]):
        part = values[:, 128 * tile : 128 * tile + 128]
        if stride == 1:
            ref[tile, start : start + count, :] = part
        else:
            ref[tile, pl.ds(start, count, stride=stride), :] = part


def get_rows(ref, start, count):
    parts = [ref[tile, start : start + count, :] for tile in range(ref.shape[0])]
    return parts[0] if len(parts) == 1 else jnp.concatenate(parts, axis=1)


def roll_lanes(values, shift):
    width = values.shape[-1]
    shift = shift % width
    if shift == 0:
        return values
    return pltpu.roll(values, shift, values.ndim - 1)


def message_places():
    places = [[(p, 18 * p, 18, 0) for p in range(7)]]
    places.append([(7 + p, 18 * p, 18, 0) for p in range(5)] + [(12 + p, 90 + 12 * p, 12, 0) for p in range(3)])
    places.append([(15 + p, 12 * p, 12, 0) for p in range(10)] + [(35, 120, 8, 0)])
    places.append([(25 + p, 12 * p, 12, 0) for p in range(10)] + [(35, 120, 4, 8)])
    return places


def pack_kernel(devices, velocity_ref, cotangent_ref, send_ref):
    length = velocity_ref.shape[3]
    planes = [velocity_ref[c, 2 + z].astype(F32) for c in range(3) for z in range(DEPTH)]
    planes += [velocity_ref[c, z].astype(F32) for c in range(3) for z in (0, 1, 6, 7)]
    planes += [cotangent_ref[c, z] for c in range(3) for z in range(DEPTH)]
    groups = []
    for places in message_places():
        members = []
        for plane, first, lanes, skipped in places:
            halo = 5 if plane < 12 else 2
            members.append((roll_lanes(planes[plane], first - skipped + halo), first))
        groups.append(members)
    lane = lax.broadcasted_iota(jnp.int32, (ROWS, length), 1)

    def one(dest):
        place = lane - ROWS * dest
        place = jnp.where(place < 0, place + length, place)
        done = []
        for members in groups:
            mixed = members[0][0]
            for values, first in members[1:]:
                mixed = jnp.where(place < first, mixed, values)
            if isinstance(dest, int):
                moved = roll_lanes(mixed, -ROWS * dest)
            else:
                moved = pltpu.roll(mixed, length - ROWS * dest, 1)
            done.append(moved[:, 0:128])
        for pair in range(2):
            both = jnp.concatenate([done[2 * pair], done[2 * pair + 1]], axis=0)
            send_ref[dest, 16 * pair : 16 * pair + 16, :] = both.astype(BF16)

    if devices <= 16:
        for dest in range(devices):
            one(dest)
    else:

        def body(dest, carry):
            one(dest)
            return carry

        lax.fori_loop(0, devices, body, 0)


def fill_weights(conv_in_ref, conv_mid_ref, conv_out_ref, scratch, matrices, rows_first):
    in_t, mid, out = scratch
    in_t[...] = jnp.zeros_like(in_t)
    for i in range(9):
        for p in range(3):
            taps = 0.5 * conv_in_ref[i, p].astype(F32)
            if rows_first:
                in_t[pl.ds(32 * p + i, 3, stride=9), 0:HIDDEN] = taps
            else:
                in_t[pl.ds(9 * p + i, 3, stride=32), 0:HIDDEN] = taps
    for p in range(3):
        for q in range(3):
            a, b = (p, q) if rows_first else (q, p)
            mid[HIDDEN * a : HIDDEN * a + HIDDEN, HIDDEN * b : HIDDEN * b + HIDDEN] = 0.5 * conv_mid_ref[p, q].astype(F32)
            out[40 * a : 40 * a + WEIGHTS, HIDDEN * b : HIDDEN * b + HIDDEN] = SPREAD * conv_out_ref[p, q].astype(F32)
    matrices[0][...] = in_t[...].T[0:HIDDEN].astype(BF16)
    matrices[1][...] = mid[...].astype(BF16)
    matrices[2][...] = out[...].astype(BF16)


def angle(coords, offset):
    return (coords + offset).astype(F32) * (2.0 * math.pi / DOMAIN)


def row_numbers(length, total):
    rows = lax.axis_index("gx") * ROWS - 8 + lax.broadcasted_iota(jnp.int32, (SPAN, length), 0)
    rows = jnp.where(rows < 0, rows + total, rows)
    return jnp.where(rows >= total, rows - total, rows)


def fill_tables(offsets_ref, table_ref, total):
    length = table_ref.shape[2]
    lanes = lax.broadcasted_iota(jnp.int32, (8, length), 1)
    layers = lax.broadcasted_iota(jnp.int32, (8, length), 0)
    rows = row_numbers(length, total)
    for axis in range(3):
        parts = [layers] if axis == 2 else [lanes, rows]
        coords = jnp.concatenate(parts, axis=0)
        turn = angle(coords, offsets_ref[axis])
        table_ref[2 * axis, 0 : turn.shape[0], :] = jnp.sin(turn)
        table_ref[2 * axis + 1, 0 : turn.shape[0], :] = jnp.cos(turn)


def fill_inputs(planes, u_ref, table_ref, row0, count, rows_first):
    length = u_ref.shape[3]

    def put(z, channel, q, values):
        put_rows(planes, z * count * INPUT_PITCH + 9 * q + channel, count, INPUT_PITCH, values)

    zero = jnp.zeros((DEPTH * count, length), F32)
    for spare in range(27, 32):
        put_rows(planes, spare, DEPTH * count, INPUT_PITCH, zero)
    row_axis, lane_axis = (1, 0) if rows_first else (0, 1)
    for part in range(2):
        rows = table_ref[2 * row_axis + part, 8 + row0 : 8 + row0 + count, :]
        row_of_lanes = table_ref[2 * lane_axis + part, 0:1, :]
        for z in range(DEPTH):
            layer = jnp.broadcast_to(table_ref[4 + part, z : z + 1, :], (count, length))
            for q in range(3):
                put(z, 3 + 2 * row_axis + part, q, rows)
                put(z, 7 + part, q, layer)
        for q in range(3):
            lanes = jnp.broadcast_to(roll_lanes(row_of_lanes, 1 - q), (count, length))
            for z in range(DEPTH):
                put(z, 3 + 2 * lane_axis + part, q, lanes)
    for c in range(3):
        for z in range(DEPTH):
            values = u_ref[c, 2 + z, row0 : row0 + count, :]
            for q in range(3):
                put(z, c, q, roll_lanes(values, 1 - q))


def gelu_of_half(half):
    return half + half * jnp.tanh(half * (GELU_LINEAR + GELU_CUBIC * (half * half)))


def spread(values, ref, row):
    length = values.shape[1] // DEPTH
    values = values.astype(BF16)
    ref[row, HIDDEN : 2 * HIDDEN, :] = values
    for z in range(DEPTH):
        lanes = slice(z * length, (z + 1) * length)
        ref[row, 0:HIDDEN, lanes] = roll_lanes(values[:, lanes], 1)
        ref[row, 2 * HIDDEN :, lanes] = roll_lanes(values[:, lanes], -1)


def tap_sums(matrix, ref, first, last, block, part, carry, emit):
    def body(step, state):
        base = first + step * block
        older = carry[0]
        newer = carry[1]
        for j in range(block):
            product = jnp.dot(matrix, ref[base + j], preferred_element_type=F32)
            emit(base + j, older + product[2 * part : 3 * part])
            older = newer + product[part : 2 * part]
            newer = product[0:part]
        carry[0] = older
        carry[1] = newer
        return state

    lax.fori_loop(0, (last - first) // block, body, 0)


def network(planes, stacked, first_ref, second_ref, carry_mid, carry_out, matrices, raw_ref, count, blocks, row0):
    length = stacked.shape[2] // DEPTH
    lanes = DEPTH * length
    matrix_in, matrix_mid, matrix_out = (m[...] for m in matrices)

    def stack(row):
        for z in range(DEPTH):
            start = (z * count + row) * INPUT_PITCH
            stacked[row, :, z * length : (z + 1) * length] = get_rows(planes, start, 32).astype(BF16)

    def first_row(row):
        operand = stacked[pl.ds(row, 3)].reshape(96, lanes)
        spread(gelu_of_half(jnp.dot(matrix_in, operand, preferred_element_type=F32)), first_ref, row)

    def emit_second(row, values):
        spread(gelu_of_half(values), second_ref, row)

    def emit_raw(row, values):
        for z in range(DEPTH):
            part = values[0:WEIGHTS, z * length : (z + 1) * length]
            for tile in range(lane_tiles(length)):
                raw_ref[tile, pl.ds(z * SPAN + row0 + row - 4, WEIGHTS, stride=WEIGHT_PITCH), :] = part[
                    :, 128 * tile : 128 * tile + 128
                ]

    if blocks is not None:
        for row in range(count):
            stack(row)

        def first_body(step, state):
            for j in range(blocks[0]):
                first_row(step * blocks[0] + j)
            return state

        lax.fori_loop(0, (count - 2) // blocks[0], first_body, 0)
        tap_sums(matrix_mid, first_ref, 0, count - 2, blocks[1], HIDDEN, carry_mid, emit_second)
        tap_sums(matrix_out, second_ref, 2, count - 2, blocks[2], 40, carry_out, emit_raw)
        return

    def rolling_sums(matrix, ref, first, part, emit):
        older = newer = None
        row = first
        while True:
            product = jnp.dot(matrix, ref[row], preferred_element_type=F32)
            if older is not None:
                emit(row, older + product[2 * part : 3 * part])
            older = None if newer is None else newer + product[part : 2 * part]
            newer = product[0:part]
            row += 1
            yield

    mid_rows = rolling_sums(matrix_mid, first_ref, 0, HIDDEN, emit_second)
    out_rows = rolling_sums(matrix_out, second_ref, 2, 40, emit_raw)
    stack(0)
    stack(1)
    for step in range(count - 2 + LAGS[1]):
        if step < count - 2:
            stack(step + 2)
            first_row(step)
        if LAGS[0] <= step < count - 2 + LAGS[0]:
            next(mid_rows)
        if LAGS[1] + 2 <= step:
            next(out_rows)


def at(ref, k, z, row, count):
    return get_rows(ref, k * WEIGHT_PITCH + z * SPAN + row, count)


def nearby(ref, c, z, row, count, direction, row_direction, steps):
    if direction == 2:
        return {t: ref[c, 2 + z + t, row : row + count, :] for t in steps}
    if direction == row_direction:
        return {t: ref[c, 2 + z, row + t : row + t + count, :] for t in steps}
    centre = ref[c, 2 + z, row : row + count, :]
    return {t: roll_lanes(centre, -t) for t in steps}


def speeds(ref, z, row, count, direction, row_direction):
    u = nearby(ref, direction, z, row, count, direction, row_direction, (-1, 0, 1))
    return 0.5 * (u[0] + u[1]), 0.5 * (u[0] + u[-1])


def advect(u_ref, w_ref, row, count, row_direction, from_raw, emit):
    for z in range(DEPTH):
        pace = [speeds(u_ref, z, row, count, d, row_direction) for d in range(3)]
        for c in range(3):
            change = None
            for d in range(3):
                taps = [at(w_ref, 12 * c + 4 * d + s, z, row, count) for s in range(4)]
                if from_raw:
                    mean = 0.25 * ((taps[0] + taps[1]) + (taps[2] + taps[3]))
                    outer, inner = BASE_TAPS[0] - mean, BASE_TAPS[1] - mean
                    for s in range(4):
                        taps[s] = (taps[s] + (inner if s in (1, 2) else outer)).astype(BF16).astype(F32)
                        put_rows(w_ref, (12 * c + 4 * d + s) * WEIGHT_PITCH + z * SPAN + row, count, 1, taps[s])
                u = nearby(u_ref, c, z, row, count, d, row_direction, (-2, -1, 0, 1, 2))
                up = (taps[0] * u[-1] + taps[1] * u[0]) + (taps[2] * u[1] + taps[3] * u[2])
                down = (taps[0] * u[-2] + taps[1] * u[-1]) + (taps[2] * u[0] + taps[3] * u[1])
                term = pace[d][0] * up - pace[d][1] * down
                change = term if change is None else change + term
            centre = u_ref[c, 2 + z, row : row + count, :]
            emit(c, z, row, count, centre - STEP_SIZE * change)


def y_kernel(
    total,
    offsets_ref,
    even_ref,
    odd_ref,
    velocity_ref,
    conv_in_ref,
    conv_mid_ref,
    conv_out_ref,
    stencil_ref,
    start_ref,
    middle_ref,
    table_ref,
    x_in_ref,
    x_mid_ref,
    x_out_ref,
    planes,
    stacked,
    first_ref,
    second_ref,
    carry_mid,
    carry_out,
    in_ref,
    mid_ref,
    out_ref,
    in_wide,
    mid_wide,
    out_wide,
):
    wide = (in_wide, mid_wide, out_wide)
    fill_tables(offsets_ref, table_ref, total)
    fill_weights(conv_in_ref, conv_mid_ref, conv_out_ref, wide, (in_ref, mid_ref, out_ref), True)
    fill_weights(conv_in_ref, conv_mid_ref, conv_out_ref, wide, (x_in_ref, x_mid_ref, x_out_ref), False)
    is_even = lax.rem(lax.axis_index("gx"), 2) == 0
    for c in range(3):
        for z in range(2 * DEPTH):
            pair = even_ref[c, z].astype(F32)
            other = odd_ref[c, z].astype(F32)
            start_ref[c, z, 0:8, :] = jnp.where(is_even, other, pair)
            start_ref[c, z, 16:24, :] = jnp.where(is_even, pair, other)
    for c in range(3):
        for z in range(2 * DEPTH):
            start_ref[c, z, 8:16, :] = velocity_ref[c, z].astype(F32)
    fill_inputs(planes, start_ref, table_ref, 1, 22, True)
    network(
        planes,
        stacked,
        first_ref,
        second_ref,
        carry_mid,
        carry_out,
        (in_ref, mid_ref, out_ref),
        stencil_ref,
        22,
        None if table_ref.shape[2] <= 128 else (5, 5, 6),
        4,
    )

    def emit(c, z, row, count, values):
        middle_ref[c, 2 + z, row : row + count, :] = values

    for row in (4, 12):
        advect(start_ref, stencil_ref, row, 8, 1, True, emit)
    for c in range(3):
        for z in (0, 1, 6, 7):
            middle_ref[c, z] = start_ref[c, z]


def adjoint_terms(u_ref, w_ref, g_ref, z, row, count, direction, put, grads):
    up_speed, down_speed = speeds(u_ref, z, row, count, direction, 1)
    into_up = None
    parts = []
    for c in range(3):
        scaled = -STEP_SIZE * g_ref[c, z, row : row + count, :]
        u = nearby(u_ref, c, z, row, count, direction, 1, (-2, -1, 0, 1, 2))
        h_up = scaled * up_speed
        h_down = scaled * down_speed
        if grads is not None:
            for s in range(4):
                grads(12 * c + 4 * direction + s, z, h_up * u[s - 1] - h_down * u[s - 2])
        if put is None:
            continue
        w = [at(w_ref, 12 * c + 4 * direction + s, z, row, count) for s in range(4)]
        up = (w[0] * u[-1] + w[1] * u[0]) + (w[2] * u[1] + w[3] * u[2])
        down = (w[0] * u[-2] + w[1] * u[-1]) + (w[2] * u[0] + w[3] * u[1])
        if into_up is None:
            into_up = scaled * up
            into_down = scaled * down
        else:
            into_up = into_up + scaled * up
            into_down = into_down + scaled * down
        parts.append(
            {
                -2: -h_down * w[0],
                -1: h_up * w[0] - h_down * w[1],
                0: h_up * w[1] - h_down * w[2],
                1: h_up * w[2] - h_down * w[3],
                2: h_up * w[3],
            }
        )
    if put is not None:
        own = parts[direction]
        own[0] = own[0] + 0.5 * (into_up - into_down)
        own[1] = own[1] + 0.5 * into_up
        own[-1] = own[-1] - 0.5 * into_down
        for c in range(3):
            put(c, parts[c])


def x_kernel(
    received_ref,
    stencil_ref,
    start_ref,
    middle_ref,
    table_ref,
    in_ref,
    mid_ref,
    out_ref,
    final_ref,
    grads_ref,
    planes,
    stacked,
    first_ref,
    second_ref,
    carry_mid,
    carry_out,
    own_ref,
    turned_ref,
    back_ref,
    raw_ref,
    next_ref,
    block_ref,
):
    length = start_ref.shape[3]

    def group(g):
        half = received_ref[:, 16 * (g // 2) : 16 * (g // 2) + 16, :].astype(F32)
        half = half[:, 8 * (g % 2) : 8 * (g % 2) + 8, :]
        return half.reshape(length, 128).T

    ghost_layers = [(c, z) for c in range(3) for z in (0, 1, 6, 7)]
    targets = [(own_ref, c, 2 + z, 3) for c in range(3) for z in range(DEPTH)]
    targets += [(own_ref, c, z, 6) for c, z in ghost_layers]
    targets += [(turned_ref, c, z, 6) for c in range(3) for z in range(DEPTH)]
    for g, places in enumerate(message_places()):
        block_ref[...] = group(g)
        for plane, first, lanes, skipped in places:
            ref, c, z, row = targets[plane]
            ref[c, z, row + skipped : row + skipped + lanes, :] = block_ref[first : first + lanes, :]

    for c in range(3):
        for z in range(DEPTH):
            back_ref[c, z, 8:16, :] = turned_ref[c, z, 8:16, :]

    def keep(k, z, values):
        put_rows(raw_ref, k * WEIGHT_PITCH + z * SPAN, ROWS, 1, values)

    for direction in range(3):
        blocks = ((8, 8, keep), (6, 2, None), (16, 2, None)) if direction == 1 else ((8, 8, keep),)
        for row, count, grads in blocks:
            for z in range(DEPTH):

                def put(c, parts):
                    if direction == 0:
                        total_part = parts[0]
                        for t in (-2, -1, 1, 2):
                            total_part = total_part + roll_lanes(parts[t], t)
                        back_ref[c, z, 8:16, :] += total_part
                    elif direction == 2:
                        for t in (-2, -1, 0, 1, 2):
                            if 0 <= z + t < DEPTH:
                                back_ref[c, z + t, 8:16, :] += parts[t]
                    else:
                        for t in (-2, -1, 0, 1, 2):
                            back_ref[c, z, row + t : row + t + count, :] += parts[t]

                adjoint_terms(middle_ref, stencil_ref, turned_ref, z, row, count, direction, put, grads)

    def finish(k, z, values):
        later = get_rows(raw_ref, k * WEIGHT_PITCH + z * SPAN, ROWS)
        grads_ref[k, z] = (later + values).astype(BF16)

    for direction in range(3):
        for z in range(DEPTH):
            adjoint_terms(start_ref, stencil_ref, back_ref, z, 8, 8, direction, None, finish)

    fill_inputs(planes, own_ref, table_ref, 3, 18, False)
    network(
        planes,
        stacked,
        first_ref,
        second_ref,
        carry_mid,
        carry_out,
        (in_ref, mid_ref, out_ref),
        raw_ref,
        18,
        None if table_ref.shape[2] <= 128 else (4, 4, 7),
        6,
    )

    def emit_middle(c, z, row, count, values):
        next_ref[c, 2 + z, row : row + count, :] = values

    for row, count in ((6, 8), (14, 4)):
        advect(own_ref, raw_ref, row, count, 0, True, emit_middle)
    for c, z in ghost_layers:
        next_ref[c, z, 8:16, :] = own_ref[c, z, 8:16, :]

    def emit_final(c, z, row, count, values):
        final_ref[c, z] = values

    advect(next_ref, raw_ref, 8, 8, 0, False, emit_final)


def network_scratch(count, length):
    lanes = DEPTH * length
    return [
        pltpu.VMEM((lane_tiles(length), DEPTH * count * INPUT_PITCH, 128), F32),
        pltpu.VMEM((count, 32, lanes), BF16),
        pltpu.VMEM((count - 2, 3 * HIDDEN, lanes), BF16),
        pltpu.VMEM((count - 2, 3 * HIDDEN, lanes), BF16),
        pltpu.VMEM((2, HIDDEN, lanes), F32),
        pltpu.VMEM((2, 40, lanes), F32),
    ]


def on_device(velocity, offsets, conv_in, conv_mid, conv_out, cotangent):
    devices = lax.axis_size("gx")
    length = velocity.shape[3]
    assert velocity.shape[2] == ROWS and velocity.shape[1] == 2 * DEPTH and length == ROWS * devices
    pairs = [(i, i ^ 1) for i in range(devices)]
    others = [(i, (i + 1) % devices if i % 2 else (i - 1) % devices) for i in range(devices)]
    vmem = pl.BlockSpec(memory_space=pltpu.VMEM)
    smem = pl.BlockSpec(memory_space=pltpu.SMEM)
    in_taps = jnp.transpose(conv_in, (1, 2, 3, 0))
    mid_taps = jnp.transpose(conv_mid, (2, 3, 0, 1))
    out_taps = jnp.transpose(conv_out, (2, 3, 0, 1))
    slab = (3, 2 * DEPTH, SPAN, length)
    weights = (lane_tiles(length), WEIGHTS * WEIGHT_PITCH, 128)
    matrices = (((HIDDEN, 96), BF16), ((3 * HIDDEN, 3 * HIDDEN), BF16), ((120, 3 * HIDDEN), BF16))
    local = [pltpu.with_memory_space_constraint(a, pltpu.HBM) for a in (velocity, in_taps, mid_taps, out_taps)]
    send = pl.pallas_call(
        functools.partial(pack_kernel, devices),
        out_shape=jax.ShapeDtypeStruct((devices, PACKED, 128), BF16),
        in_specs=[vmem] * 2,
        out_specs=vmem,
        compiler_params=pltpu.CompilerParams(vmem_limit_bytes=24 << 20),
        name="pack",
    )(local[0], pltpu.with_memory_space_constraint(cotangent, pltpu.HBM))
    moving, send = lax.optimization_barrier((velocity, send))
    received = lax.all_to_all(send, "gx", 0, 0)
    odd = lax.ppermute(moving, "gx", others)
    even = lax.ppermute(moving, "gx", pairs)
    limit = pltpu.CompilerParams(vmem_limit_bytes=(24 if length <= 128 else 61) << 20)
    stencil, start, middle, *tables = pl.pallas_call(
        functools.partial(y_kernel, length),
        out_shape=tuple(
            jax.ShapeDtypeStruct(*shape)
            for shape in ((weights, F32), (slab, F32), (slab, F32), ((6, 8 + SPAN, length), F32)) + matrices
        ),
        in_specs=[smem] + [vmem] * 6,
        out_specs=(vmem,) * 7,
        scratch_shapes=network_scratch(22, length)
        + [pltpu.VMEM(*shape) for shape in matrices]
        + [
            pltpu.VMEM((96, 128), F32),
            pltpu.VMEM((3 * HIDDEN, 3 * HIDDEN), F32),
            pltpu.VMEM((120, 3 * HIDDEN), F32),
        ],
        compiler_params=limit,
        cost_estimate=pl.CostEstimate(flops=4 * 10**9, transcendentals=10**6, bytes_accessed=10**7),
        name="y_slab",
    )(pltpu.with_memory_space_constraint(offsets, pltpu.HBM), even, odd, *local)
    final_state, weight_grads = pl.pallas_call(
        x_kernel,
        out_shape=(
            jax.ShapeDtypeStruct((3, DEPTH, ROWS, length), F32),
            jax.ShapeDtypeStruct((WEIGHTS, DEPTH, ROWS, length), BF16),
        ),
        in_specs=[vmem] * 8,
        out_specs=(vmem, vmem),
        scratch_shapes=network_scratch(18, length)
        + [
            pltpu.VMEM(slab, F32),
            pltpu.VMEM((3, DEPTH, SPAN, length), F32),
            pltpu.VMEM((3, DEPTH, SPAN, length), F32),
            pltpu.VMEM(weights, F32),
            pltpu.VMEM(slab, F32),
            pltpu.VMEM((128, length), F32),
        ],
        compiler_params=limit,
        cost_estimate=pl.CostEstimate(flops=3 * 10**9, transcendentals=10**6, bytes_accessed=10**7),
        name="x_slab",
    )(received, stencil, start, middle, *tables)
    return (final_state, weight_grads)


def solution(mesh):
    return jax.shard_map(
        on_device,
        mesh=mesh,
        in_specs=(
            P(None, "groups", "gx", None),
            P("groups"),
            P(),
            P(),
            P(),
            P(None, "groups", "gx", None),
        ),
        out_specs=(P(None, "groups", "gx", None), P(None, "groups", "gx", None)),
        check_vma=False,
    )
```

```python
import functools
import math

import jax
import jax.numpy as jnp
from jax import lax
from jax.experimental import pallas as pl
from jax.experimental.pallas import tpu as pltpu
from jax.sharding import PartitionSpec as P

DOMAIN = 1024
SPREAD = 0.25
STEP_SIZE = 0.3
BASE_TAPS = (-0.0625, 0.5625, 0.5625, -0.0625)

GELU_LINEAR = 2.0 * math.sqrt(2.0 / math.pi)
GELU_CUBIC = 4.0 * 0.044715 * GELU_LINEAR

DEPTH = 4
ROWS = 8
SPAN = 24
HIDDEN = 64
WEIGHTS = 36
INPUT_PITCH = 33
LAGS = (20, 40)
WEIGHT_PITCH = DEPTH * SPAN + 1
PACKED = 32
F32 = jnp.float32
BF16 = jnp.bfloat16


def lane_tiles(length):
    return length // 128


def put_rows(ref, start, count, stride, values):
    for tile in range(ref.shape[0]):
        part = values[:, 128 * tile : 128 * tile + 128]
        if stride == 1:
            ref[tile, start : start + count, :] = part
        else:
            ref[tile, pl.ds(start, count, stride=stride), :] = part


def get_rows(ref, start, count):
    parts = [ref[tile, start : start + count, :] for tile in range(ref.shape[0])]
    return parts[0] if len(parts) == 1 else jnp.concatenate(parts, axis=1)


def roll_lanes(values, shift):
    width = values.shape[-1]
    shift = shift % width
    if shift == 0:
        return values
    return pltpu.roll(values, shift, values.ndim - 1)


def message_places():
    places = [[(p, 18 * p, 18, 0) for p in range(7)]]
    places.append([(7 + p, 18 * p, 18, 0) for p in range(5)] + [(12 + p, 90 + 12 * p, 12, 0) for p in range(3)])
    places.append([(15 + p, 12 * p, 12, 0) for p in range(10)] + [(35, 120, 8, 0)])
    places.append([(25 + p, 12 * p, 12, 0) for p in range(10)] + [(35, 120, 4, 8)])
    return places


def pack_kernel(devices, velocity_ref, cotangent_ref, send_ref):
    length = velocity_ref.shape[3]
    planes = [velocity_ref[c, 2 + z].astype(F32) for c in range(3) for z in range(DEPTH)]
    planes += [velocity_ref[c, z].astype(F32) for c in range(3) for z in (0, 1, 6, 7)]
    planes += [cotangent_ref[c, z] for c in range(3) for z in range(DEPTH)]
    groups = []
    for places in message_places():
        members = []
        for plane, first, lanes, skipped in places:
            halo = 5 if plane < 12 else 2
            members.append((roll_lanes(planes[plane], first - skipped + halo), first))
        groups.append(members)
    lane = lax.broadcasted_iota(jnp.int32, (ROWS, length), 1)

    def one(dest):
        place = lane - ROWS * dest
        place = jnp.where(place < 0, place + length, place)
        done = []
        for members in groups:
            mixed = members[0][0]
            for values, first in members[1:]:
                mixed = jnp.where(place < first, mixed, values)
            if isinstance(dest, int):
                moved = roll_lanes(mixed, -ROWS * dest)
            else:
                moved = pltpu.roll(mixed, length - ROWS * dest, 1)
            done.append(moved[:, 0:128])
        for pair in range(2):
            both = jnp.concatenate([done[2 * pair], done[2 * pair + 1]], axis=0)
            send_ref[dest, 16 * pair : 16 * pair + 16, :] = both.astype(BF16)

    if devices <= 16:
        for dest in range(devices):
            one(dest)
    else:

        def body(dest, carry):
            one(dest)
            return carry

        lax.fori_loop(0, devices, body, 0)


def fill_weights(conv_in_ref, conv_mid_ref, conv_out_ref, scratch, matrices, rows_first):
    in_t, mid, out = scratch
    in_t[...] = jnp.zeros_like(in_t)
    for i in range(9):
        for p in range(3):
            taps = 0.5 * conv_in_ref[i, p].astype(F32)
            if rows_first:
                in_t[pl.ds(32 * p + i, 3, stride=9), 0:HIDDEN] = taps
            else:
                in_t[pl.ds(9 * p + i, 3, stride=32), 0:HIDDEN] = taps
    for p in range(3):
        for q in range(3):
            a, b = (p, q) if rows_first else (q, p)
            mid[HIDDEN * a : HIDDEN * a + HIDDEN, HIDDEN * b : HIDDEN * b + HIDDEN] = 0.5 * conv_mid_ref[p, q].astype(F32)
            out[40 * a : 40 * a + WEIGHTS, HIDDEN * b : HIDDEN * b + HIDDEN] = SPREAD * conv_out_ref[p, q].astype(F32)
    matrices[0][...] = in_t[...].T[0:HIDDEN].astype(BF16)
    matrices[1][...] = mid[...].astype(BF16)
    matrices[2][...] = out[...].astype(BF16)


def angle(coords, offset):
    return (coords + offset).astype(F32) * (2.0 * math.pi / DOMAIN)


def row_numbers(length, total):
    rows = lax.axis_index("gx") * ROWS - 8 + lax.broadcasted_iota(jnp.int32, (SPAN, length), 0)
    rows = jnp.where(rows < 0, rows + total, rows)
    return jnp.where(rows >= total, rows - total, rows)


def fill_tables(offsets_ref, table_ref, total):
    length = table_ref.shape[2]
    lanes = lax.broadcasted_iota(jnp.int32, (8, length), 1)
    layers = lax.broadcasted_iota(jnp.int32, (8, length), 0)
    rows = row_numbers(length, total)
    for axis in range(3):
        parts = [layers] if axis == 2 else [lanes, rows]
        coords = jnp.concatenate(parts, axis=0)
        turn = angle(coords, offsets_ref[axis])
        table_ref[2 * axis, 0 : turn.shape[0], :] = jnp.sin(turn)
        table_ref[2 * axis + 1, 0 : turn.shape[0], :] = jnp.cos(turn)


def fill_inputs(planes, u_ref, table_ref, row0, count, rows_first):
    length = u_ref.shape[3]

    def put(z, channel, q, values):
        put_rows(planes, z * count * INPUT_PITCH + 9 * q + channel, count, INPUT_PITCH, values)

    zero = jnp.zeros((DEPTH * count, length), F32)
    for spare in range(27, 32):
        put_rows(planes, spare, DEPTH * count, INPUT_PITCH, zero)
    row_axis, lane_axis = (1, 0) if rows_first else (0, 1)
    for part in range(2):
        rows = table_ref[2 * row_axis + part, 8 + row0 : 8 + row0 + count, :]
        row_of_lanes = table_ref[2 * lane_axis + part, 0:1, :]
        for z in range(DEPTH):
            layer = jnp.broadcast_to(table_ref[4 + part, z : z + 1, :], (count, length))
            for q in range(3):
                put(z, 3 + 2 * row_axis + part, q, rows)
                put(z, 7 + part, q, layer)
        for q in range(3):
            lanes = jnp.broadcast_to(roll_lanes(row_of_lanes, 1 - q), (count, length))
            for z in range(DEPTH):
                put(z, 3 + 2 * lane_axis + part, q, lanes)
    for c in range(3):
        for z in range(DEPTH):
            values = u_ref[c, 2 + z, row0 : row0 + count, :]
            for q in range(3):
                put(z, c, q, roll_lanes(values, 1 - q))


def gelu_of_half(half):
    return half + half * jnp.tanh(half * (GELU_LINEAR + GELU_CUBIC * (half * half)))


def spread(values, ref, row):
    length = values.shape[1] // DEPTH
    values = values.astype(BF16)
    ref[row, HIDDEN : 2 * HIDDEN, :] = values
    for z in range(DEPTH):
        lanes = slice(z * length, (z + 1) * length)
        ref[row, 0:HIDDEN, lanes] = roll_lanes(values[:, lanes], 1)
        ref[row, 2 * HIDDEN :, lanes] = roll_lanes(values[:, lanes], -1)


def tap_sums(matrix, ref, first, last, block, part, carry, emit):
    def body(step, state):
        base = first + step * block
        older = carry[0]
        newer = carry[1]
        for j in range(block):
            product = jnp.dot(matrix, ref[base + j], preferred_element_type=F32)
            emit(base + j, older + product[2 * part : 3 * part])
            older = newer + product[part : 2 * part]
            newer = product[0:part]
        carry[0] = older
        carry[1] = newer
        return state

    lax.fori_loop(0, (last - first) // block, body, 0)


def network(planes, stacked, first_ref, second_ref, carry_mid, carry_out, matrices, raw_ref, count, blocks, row0):
    length = stacked.shape[2] // DEPTH
    lanes = DEPTH * length
    matrix_in, matrix_mid, matrix_out = (m[...] for m in matrices)

    def stack(row):
        for z in range(DEPTH):
            start = (z * count + row) * INPUT_PITCH
            stacked[row, :, z * length : (z + 1) * length] = get_rows(planes, start, 32).astype(BF16)

    def first_row(row):
        operand = stacked[pl.ds(row, 3)].reshape(96, lanes)
        spread(gelu_of_half(jnp.dot(matrix_in, operand, preferred_element_type=F32)), first_ref, row)

    def emit_second(row, values):
        spread(gelu_of_half(values), second_ref, row)

    def emit_raw(row, values):
        for z in range(DEPTH):
            part = values[0:WEIGHTS, z * length : (z + 1) * length]
            for tile in range(lane_tiles(length)):
                raw_ref[tile, pl.ds(z * SPAN + row0 + row - 4, WEIGHTS, stride=WEIGHT_PITCH), :] = part[
                    :, 128 * tile : 128 * tile + 128
                ]

    if blocks is not None:
        for row in range(count):
            stack(row)

        def first_body(step, state):
            for j in range(blocks[0]):
                first_row(step * blocks[0] + j)
            return state

        lax.fori_loop(0, (count - 2) // blocks[0], first_body, 0)
        tap_sums(matrix_mid, first_ref, 0, count - 2, blocks[1], HIDDEN, carry_mid, emit_second)
        tap_sums(matrix_out, second_ref, 2, count - 2, blocks[2], 40, carry_out, emit_raw)
        return

    def rolling_sums(matrix, ref, first, part, emit):
        older = newer = None
        row = first
        while True:
            product = jnp.dot(matrix, ref[row], preferred_element_type=F32)
            if older is not None:
                emit(row, older + product[2 * part : 3 * part])
            older = None if newer is None else newer + product[part : 2 * part]
            newer = product[0:part]
            row += 1
            yield

    mid_rows = rolling_sums(matrix_mid, first_ref, 0, HIDDEN, emit_second)
    out_rows = rolling_sums(matrix_out, second_ref, 2, 40, emit_raw)
    stack(0)
    stack(1)
    for step in range(count - 2 + LAGS[1]):
        if step < count - 2:
            stack(step + 2)
            first_row(step)
        if LAGS[0] <= step < count - 2 + LAGS[0]:
            next(mid_rows)
        if LAGS[1] + 2 <= step:
            next(out_rows)


def at(ref, k, z, row, count):
    return get_rows(ref, k * WEIGHT_PITCH + z * SPAN + row, count)


def nearby(ref, c, z, row, count, direction, row_direction, steps):
    if direction == 2:
        return {t: ref[c, 2 + z + t, row : row + count, :] for t in steps}
    if direction == row_direction:
        return {t: ref[c, 2 + z, row + t : row + t + count, :] for t in steps}
    centre = ref[c, 2 + z, row : row + count, :]
    return {t: roll_lanes(centre, -t) for t in steps}


def speeds(ref, z, row, count, direction, row_direction):
    u = nearby(ref, direction, z, row, count, direction, row_direction, (-1, 0, 1))
    return 0.5 * (u[0] + u[1]), 0.5 * (u[0] + u[-1])


def advect(u_ref, w_ref, row, count, row_direction, from_raw, emit):
    for z in range(DEPTH):
        pace = [speeds(u_ref, z, row, count, d, row_direction) for d in range(3)]
        for c in range(3):
            change = None
            for d in range(3):
                taps = [at(w_ref, 12 * c + 4 * d + s, z, row, count) for s in range(4)]
                if from_raw:
                    mean = 0.25 * ((taps[0] + taps[1]) + (taps[2] + taps[3]))
                    outer, inner = BASE_TAPS[0] - mean, BASE_TAPS[1] - mean
                    for s in range(4):
                        taps[s] = (taps[s] + (inner if s in (1, 2) else outer)).astype(BF16).astype(F32)
                        put_rows(w_ref, (12 * c + 4 * d + s) * WEIGHT_PITCH + z * SPAN + row, count, 1, taps[s])
                u = nearby(u_ref, c, z, row, count, d, row_direction, (-2, -1, 0, 1, 2))
                up = (taps[0] * u[-1] + taps[1] * u[0]) + (taps[2] * u[1] + taps[3] * u[2])
                down = (taps[0] * u[-2] + taps[1] * u[-1]) + (taps[2] * u[0] + taps[3] * u[1])
                term = pace[d][0] * up - pace[d][1] * down
                change = term if change is None else change + term
            centre = u_ref[c, 2 + z, row : row + count, :]
            emit(c, z, row, count, centre - STEP_SIZE * change)


def y_kernel(
    total,
    offsets_ref,
    even_ref,
    odd_ref,
    velocity_ref,
    conv_in_ref,
    conv_mid_ref,
    conv_out_ref,
    stencil_ref,
    start_ref,
    middle_ref,
    table_ref,
    x_in_ref,
    x_mid_ref,
    x_out_ref,
    planes,
    stacked,
    first_ref,
    second_ref,
    carry_mid,
    carry_out,
    in_ref,
    mid_ref,
    out_ref,
    in_wide,
    mid_wide,
    out_wide,
):
    wide = (in_wide, mid_wide, out_wide)
    fill_tables(offsets_ref, table_ref, total)
    fill_weights(conv_in_ref, conv_mid_ref, conv_out_ref, wide, (in_ref, mid_ref, out_ref), True)
    fill_weights(conv_in_ref, conv_mid_ref, conv_out_ref, wide, (x_in_ref, x_mid_ref, x_out_ref), False)
    is_even = lax.rem(lax.axis_index("gx"), 2) == 0
    for c in range(3):
        for z in range(2 * DEPTH):
            pair = even_ref[c, z].astype(F32)
            other = odd_ref[c, z].astype(F32)
            start_ref[c, z, 0:8, :] = jnp.where(is_even, other, pair)
            start_ref[c, z, 16:24, :] = jnp.where(is_even, pair, other)
    for c in range(3):
        for z in range(2 * DEPTH):
            start_ref[c, z, 8:16, :] = velocity_ref[c, z].astype(F32)
    fill_inputs(planes, start_ref, table_ref, 1, 22, True)
    network(
        planes,
        stacked,
        first_ref,
        second_ref,
        carry_mid,
        carry_out,
        (in_ref, mid_ref, out_ref),
        stencil_ref,
        22,
        None if table_ref.shape[2] <= 128 else (5, 5, 6),
        4,
    )

    def emit(c, z, row, count, values):
        middle_ref[c, 2 + z, row : row + count, :] = values

    for row in (4, 12):
        advect(start_ref, stencil_ref, row, 8, 1, True, emit)
    for c in range(3):
        for z in (0, 1, 6, 7):
            middle_ref[c, z] = start_ref[c, z]


def adjoint_terms(u_ref, w_ref, g_ref, z, row, count, direction, put, grads):
    up_speed, down_speed = speeds(u_ref, z, row, count, direction, 1)
    into_up = None
    parts = []
    for c in range(3):
        scaled = -STEP_SIZE * g_ref[c, z, row : row + count, :]
        u = nearby(u_ref, c, z, row, count, direction, 1, (-2, -1, 0, 1, 2))
        h_up = scaled * up_speed
        h_down = scaled * down_speed
        if grads is not None:
            for s in range(4):
                grads(12 * c + 4 * direction + s, z, h_up * u[s - 1] - h_down * u[s - 2])
        if put is None:
            continue
        w = [at(w_ref, 12 * c + 4 * direction + s, z, row, count) for s in range(4)]
        up = (w[0] * u[-1] + w[1] * u[0]) + (w[2] * u[1] + w[3] * u[2])
        down = (w[0] * u[-2] + w[1] * u[-1]) + (w[2] * u[0] + w[3] * u[1])
        if into_up is None:
            into_up = scaled * up
            into_down = scaled * down
        else:
            into_up = into_up + scaled * up
            into_down = into_down + scaled * down
        parts.append(
            {
                -2: -h_down * w[0],
                -1: h_up * w[0] - h_down * w[1],
                0: h_up * w[1] - h_down * w[2],
                1: h_up * w[2] - h_down * w[3],
                2: h_up * w[3],
            }
        )
    if put is not None:
        own = parts[direction]
        own[0] = own[0] + 0.5 * (into_up - into_down)
        own[1] = own[1] + 0.5 * into_up
        own[-1] = own[-1] - 0.5 * into_down
        for c in range(3):
            put(c, parts[c])


def x_kernel(
    received_ref,
    stencil_ref,
    start_ref,
    middle_ref,
    table_ref,
    in_ref,
    mid_ref,
    out_ref,
    final_ref,
    grads_ref,
    planes,
    stacked,
    first_ref,
    second_ref,
    carry_mid,
    carry_out,
    own_ref,
    turned_ref,
    back_ref,
    raw_ref,
    next_ref,
    block_ref,
):
    length = start_ref.shape[3]

    def group(g):
        half = received_ref[:, 16 * (g // 2) : 16 * (g // 2) + 16, :].astype(F32)
        half = half[:, 8 * (g % 2) : 8 * (g % 2) + 8, :]
        return half.reshape(length, 128).T

    ghost_layers = [(c, z) for c in range(3) for z in (0, 1, 6, 7)]
    targets = [(own_ref, c, 2 + z, 3) for c in range(3) for z in range(DEPTH)]
    targets += [(own_ref, c, z, 6) for c, z in ghost_layers]
    targets += [(turned_ref, c, z, 6) for c in range(3) for z in range(DEPTH)]
    for g, places in enumerate(message_places()):
        block_ref[...] = group(g)
        for plane, first, lanes, skipped in places:
            ref, c, z, row = targets[plane]
            ref[c, z, row + skipped : row + skipped + lanes, :] = block_ref[first : first + lanes, :]

    for c in range(3):
        for z in range(DEPTH):
            back_ref[c, z, 8:16, :] = turned_ref[c, z, 8:16, :]

    def keep(k, z, values):
        put_rows(raw_ref, k * WEIGHT_PITCH + z * SPAN, ROWS, 1, values)

    for direction in range(3):
        blocks = ((8, 8, keep), (6, 2, None), (16, 2, None)) if direction == 1 else ((8, 8, keep),)
        for row, count, grads in blocks:
            for z in range(DEPTH):

                def put(c, parts):
                    if direction == 0:
                        total_part = parts[0]
                        for t in (-2, -1, 1, 2):
                            total_part = total_part + roll_lanes(parts[t], t)
                        back_ref[c, z, 8:16, :] += total_part
                    elif direction == 2:
                        for t in (-2, -1, 0, 1, 2):
                            if 0 <= z + t < DEPTH:
                                back_ref[c, z + t, 8:16, :] += parts[t]
                    else:
                        for t in (-2, -1, 0, 1, 2):
                            back_ref[c, z, row + t : row + t + count, :] += parts[t]

                adjoint_terms(middle_ref, stencil_ref, turned_ref, z, row, count, direction, put, grads)

    def finish(k, z, values):
        later = get_rows(raw_ref, k * WEIGHT_PITCH + z * SPAN, ROWS)
        grads_ref[k, z] = (later + values).astype(BF16)

    for direction in range(3):
        for z in range(DEPTH):
            adjoint_terms(start_ref, stencil_ref, back_ref, z, 8, 8, direction, None, finish)

    fill_inputs(planes, own_ref, table_ref, 3, 18, False)
    network(
        planes,
        stacked,
        first_ref,
        second_ref,
        carry_mid,
        carry_out,
        (in_ref, mid_ref, out_ref),
        raw_ref,
        18,
        None if table_ref.shape[2] <= 128 else (4, 4, 7),
        6,
    )

    def emit_middle(c, z, row, count, values):
        next_ref[c, 2 + z, row : row + count, :] = values

    for row, count in ((6, 12),):
        advect(own_ref, raw_ref, row, count, 0, True, emit_middle)
    for c, z in ghost_layers:
        next_ref[c, z, 8:16, :] = own_ref[c, z, 8:16, :]

    def emit_final(c, z, row, count, values):
        final_ref[c, z] = values

    advect(next_ref, raw_ref, 8, 8, 0, False, emit_final)


def network_scratch(count, length):
    lanes = DEPTH * length
    return [
        pltpu.VMEM((lane_tiles(length), DEPTH * count * INPUT_PITCH, 128), F32),
        pltpu.VMEM((count, 32, lanes), BF16),
        pltpu.VMEM((count - 2, 3 * HIDDEN, lanes), BF16),
        pltpu.VMEM((count - 2, 3 * HIDDEN, lanes), BF16),
        pltpu.VMEM((2, HIDDEN, lanes), F32),
        pltpu.VMEM((2, 40, lanes), F32),
    ]


def on_device(velocity, offsets, conv_in, conv_mid, conv_out, cotangent):
    devices = lax.axis_size("gx")
    length = velocity.shape[3]
    assert velocity.shape[2] == ROWS and velocity.shape[1] == 2 * DEPTH and length == ROWS * devices
    pairs = [(i, i ^ 1) for i in range(devices)]
    others = [(i, (i + 1) % devices if i % 2 else (i - 1) % devices) for i in range(devices)]
    vmem = pl.BlockSpec(memory_space=pltpu.VMEM)
    smem = pl.BlockSpec(memory_space=pltpu.SMEM)
    in_taps = jnp.transpose(conv_in, (1, 2, 3, 0))
    mid_taps = jnp.transpose(conv_mid, (2, 3, 0, 1))
    out_taps = jnp.transpose(conv_out, (2, 3, 0, 1))
    slab = (3, 2 * DEPTH, SPAN, length)
    weights = (lane_tiles(length), WEIGHTS * WEIGHT_PITCH, 128)
    matrices = (((HIDDEN, 96), BF16), ((3 * HIDDEN, 3 * HIDDEN), BF16), ((120, 3 * HIDDEN), BF16))
    local = [pltpu.with_memory_space_constraint(a, pltpu.HBM) for a in (velocity, in_taps, mid_taps, out_taps)]
    send = pl.pallas_call(
        functools.partial(pack_kernel, devices),
        out_shape=jax.ShapeDtypeStruct((devices, PACKED, 128), BF16),
        in_specs=[vmem] * 2,
        out_specs=vmem,
        compiler_params=pltpu.CompilerParams(vmem_limit_bytes=24 << 20),
        name="pack",
    )(local[0], pltpu.with_memory_space_constraint(cotangent, pltpu.HBM))
    moving, send = lax.optimization_barrier((velocity, send))
    received = lax.all_to_all(send, "gx", 0, 0)
    odd = lax.ppermute(moving, "gx", others)
    even = lax.ppermute(moving, "gx", pairs)
    limit = pltpu.CompilerParams(vmem_limit_bytes=(24 if length <= 128 else 61) << 20)
    stencil, start, middle, *tables = pl.pallas_call(
        functools.partial(y_kernel, length),
        out_shape=tuple(
            jax.ShapeDtypeStruct(*shape)
            for shape in ((weights, F32), (slab, F32), (slab, F32), ((6, 8 + SPAN, length), F32)) + matrices
        ),
        in_specs=[smem] + [vmem] * 6,
        out_specs=(vmem,) * 7,
        scratch_shapes=network_scratch(22, length)
        + [pltpu.VMEM(*shape) for shape in matrices]
        + [
            pltpu.VMEM((96, 128), F32),
            pltpu.VMEM((3 * HIDDEN, 3 * HIDDEN), F32),
            pltpu.VMEM((120, 3 * HIDDEN), F32),
        ],
        compiler_params=limit,
        cost_estimate=pl.CostEstimate(flops=4 * 10**9, transcendentals=10**6, bytes_accessed=10**7),
        name="y_slab",
    )(pltpu.with_memory_space_constraint(offsets, pltpu.HBM), even, odd, *local)
    final_state, weight_grads = pl.pallas_call(
        x_kernel,
        out_shape=(
            jax.ShapeDtypeStruct((3, DEPTH, ROWS, length), F32),
            jax.ShapeDtypeStruct((WEIGHTS, DEPTH, ROWS, length), BF16),
        ),
        in_specs=[vmem] * 8,
        out_specs=(vmem, vmem),
        scratch_shapes=network_scratch(18, length)
        + [
            pltpu.VMEM(slab, F32),
            pltpu.VMEM((3, DEPTH, SPAN, length), F32),
            pltpu.VMEM((3, DEPTH, SPAN, length), F32),
            pltpu.VMEM(weights, F32),
            pltpu.VMEM(slab, F32),
            pltpu.VMEM((128, length), F32),
        ],
        compiler_params=limit,
        cost_estimate=pl.CostEstimate(flops=3 * 10**9, transcendentals=10**6, bytes_accessed=10**7),
        name="x_slab",
    )(received, stencil, start, middle, *tables)
    return (final_state, weight_grads)


def solution(mesh):
    return jax.shard_map(
        on_device,
        mesh=mesh,
        in_specs=(
            P(None, "groups", "gx", None),
            P("groups"),
            P(),
            P(),
            P(),
            P(None, "groups", "gx", None),
        ),
        out_specs=(P(None, "groups", "gx", None), P(None, "groups", "gx", None)),
        check_vma=False,
    )
```
